32 devices in a mesh: groups: 2 (over x), seq: 16 (over z, y, core).
Axes of the slice: x: 2, y: 2, z: 4, core: 2. Of those that a mesh axis runs over, the one named last changes fastest.
Arguments:
- proj: bfloat16 [4096, 12288], P(('groups', 'seq')), parts along dimension 0, may hold values from -6 to 6
- short_weight: float32 [7, 12288], replicated, may hold values from -2 to 2
- residues: float32 [16, 4096], replicated, may hold values from -10 to 10
- rates: float32 [16, 4096], replicated, may hold values from 0.00024414062 to 0.05
- skip: float32 [4096], replicated, may hold values from -0.75 to 0.75
- grad_out: bfloat16 [4096, 4096], P(('groups', 'seq')), parts along dimension 0, may hold values from -0.3125 to 0.3125
Outputs:
- gated_output: bfloat16 [4096, 4096], P(('groups', 'seq')), parts along dimension 0
- filter_grad: float32 [4096, 4096], P(('groups', 'seq')), parts along dimension 0
The draws below stay inside these ranges and needn't reach their ends.
There are 2 independent parts, one for each index of `groups`. The reference program is written for one: setup_inputs(seed, part) draws one part's arguments, and reference() takes and returns one part's arrays. A program takes and returns all parts, laid end to end along the dimension named above; an argument that names none is the same for every part. Nothing has to cross between parts.
All inputs are finite; a program needn't handle non-finite values.
Results may differ from the reference program's by a relative error of at most 0.0085.
Values may be sent and summed in bfloat16 or wider, within the bound.
No kernel may reach another device: no remote copies, remote signals or barrier semaphores. Data moves between devices by JAX's collectives and lax.ppermute only.
A program may use at most 128 MiB of HBM per device.

```python
import math
import jax
import jax.numpy as jnp
from jax import lax

C = 4096
MODES = 16
TAPS = 7
SEQ_LEN = 2048


def modal_draw(key):
    base = jax.random.fold_in(key, 523)
    choose_key, spread_key, amp_key = jax.random.split(base, 3)
    fast = jax.random.randint(choose_key, (MODES, C), 0, 2) == 1
    spread = jax.random.uniform(spread_key, (MODES, C), jnp.float32)
    fast_rate = 0.02 * jnp.exp(spread * math.log(2.5))
    slow_rate = 0.5 / SEQ_LEN * jnp.exp(spread * math.log(8.0))
    rate_values = jnp.where(fast, fast_rate, slow_rate).astype(jnp.float32)
    raw = jnp.clip(0.35 * jax.random.normal(amp_key, (MODES, C), jnp.float32), -2.0, 2.0)
    root = jnp.sqrt(rate_values)
    total = jnp.sum(raw * root, axis=0)
    weight_sum = jnp.sum(rate_values, axis=0)
    residue_values = raw - root * (total / weight_sum)[None, :]
    return (rate_values, residue_values)


def draw_rates(key, part):
    return modal_draw(key)[0]


def draw_residues(key, part):
    return modal_draw(key)[1]


def draw_proj(key, part):
    keys = jax.random.split(jax.random.fold_in(key, 311), 7)
    positions = jnp.arange(SEQ_LEN, dtype=jnp.float32)[:, None]
    query_part = jnp.clip(jax.random.normal(keys[0], (SEQ_LEN, C), jnp.float32), -6.0, 6.0)
    key_noise = 0.3 * jnp.clip(jax.random.normal(keys[1], (SEQ_LEN, C), jnp.float32), -6.0, 6.0)
    value_noise = 0.3 * jnp.clip(jax.random.normal(keys[2], (SEQ_LEN, C), jnp.float32), -6.0, 6.0)
    low_period = 10.0
    high_period = 100.0
    low_offset = 0.8
    high_offset = 1.6
    periods = low_period * jnp.exp(jax.random.uniform(keys[3], (3, C), jnp.float32) * math.log(high_period / low_period))
    phases = jax.random.uniform(keys[4], (3, C), jnp.float32, 0.0, 2.0 * math.pi)
    key_part = key_noise
    for wave in range(3):
        omega = 2.0 * math.pi / periods[wave]
        key_part = key_part + 0.8 * jnp.cos(positions * omega[None, :] + phases[wave][None, :])
    signs = jnp.where(jax.random.randint(keys[5], (C,), 0, 2) == 1, 1.0, -1.0).astype(jnp.float32)
    magnitude = low_offset + (high_offset - low_offset) * jax.random.uniform(keys[6], (C,), jnp.float32)
    value_part = (signs * magnitude)[None, :] + value_noise
    return jnp.concatenate([query_part, key_part, value_part], axis=1).astype(jnp.bfloat16)


def steps_of(key, shape, pieces, low, high):
    factor_of, own = 1.0, jax.random.fold_in(key, 6)
    for dim, parts in pieces:
        draws = jnp.exp(jax.random.uniform(jax.random.fold_in(own, dim), (parts,), jnp.float32, low / len(pieces), high / len(pieces)))
        factor_of = factor_of * jnp.repeat(draws, shape[dim] // parts).reshape([-1 if axis == dim else 1 for axis in range(len(shape))])
    return factor_of


def bell_draw(key, dims, deviation, most, pieces=(), kind=jnp.bfloat16):
    level = steps_of(key, dims, pieces, -0.22, 0.18) if pieces else 1.0
    values = jax.random.normal(key, dims, jnp.float32) * deviation * level
    return jnp.minimum(jnp.maximum(values, -most), most).astype(kind)


def setup_inputs(seed: int = 0, part: int = 0) -> dict:
    seeds = jax.random.split(jax.random.key(seed), 7)
    part_keys = jax.random.split(jax.random.fold_in(seeds[6], part), 7)
    proj = draw_proj(jax.random.fold_in(jax.random.fold_in(seeds[6], part), 71), part)
    short_weight = bell_draw(seeds[1], (TAPS, 3 * C), TAPS ** -0.5, 2.0, (), jnp.float32)
    residues = draw_residues(jax.random.fold_in(seeds[6], 71), part)
    rates = draw_rates(jax.random.fold_in(seeds[6], 71), part)
    skip = bell_draw(seeds[4], (C,), 0.05, 0.75, (), jnp.float32)
    grad_out = bell_draw(part_keys[5], (SEQ_LEN, C), (1.0 / SEQ_LEN ** 0.5), 0.3125, ((0, 16),))
    return dict(proj=proj, short_weight=short_weight, residues=residues, rates=rates, skip=skip, grad_out=grad_out)


def reference(proj, short_weight, residues, rates, skip, grad_out):
    length = SEQ_LEN
    width = math.gcd(C, 256)
    blocks = C // width
    streams = proj.reshape(length, 3, blocks, width).transpose(2, 1, 0, 3)
    cotangent = grad_out.reshape(length, blocks, width).transpose(1, 0, 2)
    weights = short_weight.reshape(TAPS, 3, blocks, width).transpose(2, 0, 1, 3)
    residue_blocks = residues.reshape(MODES, blocks, width).transpose(1, 0, 2)
    rate_blocks = rates.reshape(MODES, blocks, width).transpose(1, 0, 2)
    skip_blocks = skip.reshape(blocks, width)

    def one_block(items):
        stream_block, cotangent_block, weight_block, residue_block, rate_block, skip_block = items
        padded = jnp.pad(stream_block.astype(jnp.float32), ((0, 0), (TAPS - 1, 0), (0, 0)))
        filtered = jnp.zeros((3, length, width), jnp.float32)
        for tap_index in range(TAPS):
            offset = TAPS - 1 - tap_index
            filtered = filtered + weight_block[tap_index][:, None, :] * padded[:, offset:offset + length, :]
        query_part = filtered[0]
        mixed = (filtered[1] * filtered[2]).astype(jnp.bfloat16)
        scaled = (query_part * cotangent_block.astype(jnp.float32)).astype(jnp.bfloat16)
        positions = jnp.arange(length, dtype=jnp.float32)[:, None]
        kernel = jnp.zeros((length, width), jnp.float32)
        for mode_index in range(MODES):
            rate_row = rate_block[mode_index][None, :]
            kernel = kernel + residue_block[mode_index][None, :] * jnp.sqrt(rate_row) * jnp.exp(-rate_row * positions)
        padded_length = 2 * length
        spec_mixed = jnp.fft.rfft(mixed.astype(jnp.float32), n=padded_length, axis=0)
        spec_kernel = jnp.fft.rfft(kernel, n=padded_length, axis=0)
        conv = jnp.fft.irfft(spec_mixed * spec_kernel, n=padded_length, axis=0)[:length]
        conv = (conv + skip_block[None, :] * mixed.astype(jnp.float32)).astype(jnp.bfloat16)
        gated = (query_part * conv.astype(jnp.float32)).astype(jnp.bfloat16)
        spec_scaled = jnp.fft.rfft(scaled.astype(jnp.float32), n=padded_length, axis=0)
        lagged = jnp.fft.irfft(jnp.conj(spec_mixed) * spec_scaled, n=padded_length, axis=0)[:length]
        return (gated, lagged.astype(jnp.float32))
    gated, lagged = lax.map(one_block, (streams, cotangent, weights, residue_blocks, rate_blocks, skip_blocks))
    gated_output = gated.transpose(1, 0, 2).reshape(length, C)
    filter_grad = lagged.transpose(1, 0, 2).reshape(length, C)
    return (gated_output, filter_grad)
```

```python
import functools
import math

import jax
import jax.numpy as jnp
from jax import lax
from jax.experimental import pallas as pl
from jax.experimental.pallas import tpu as pltpu
from jax.sharding import PartitionSpec as P

HIGH_PRECISION = lax.Precision.HIGH
LANES = 128
HALO = 8
FINE_PRODUCT = 256


def make_tables(devices, rows):
    length = devices * rows
    halves = jnp.arange(2, dtype=jnp.int32)
    coarse = jnp.arange(devices, dtype=jnp.int32)
    fine_pos = jnp.arange(rows, dtype=jnp.int32)
    outer_turn = (
        coarse[None, None, :] * (2 * coarse[None, :, None] + halves[:, None, None]) % (2 * devices)
    )
    outer_angle = -math.pi / devices * outer_turn.astype(jnp.float32)
    twist_turn = (
        fine_pos[None, None, :] * (2 * coarse[None, :, None] + halves[:, None, None]) % (2 * length)
    )
    twist_angle = -math.pi / length * twist_turn.astype(jnp.float32)
    inner_turn = fine_pos[:, None] * fine_pos[None, :] % rows
    inner_angle = -2.0 * math.pi / rows * inner_turn.astype(jnp.float32)
    outer_stack = jnp.stack([jnp.cos(outer_angle), jnp.sin(outer_angle)])
    inverse_outer = outer_stack * (0.5 / length)
    inner_cos = jnp.cos(inner_angle)
    inner_sin = jnp.sin(inner_angle)
    forward_inner = jnp.stack(
        [jnp.stack([inner_cos, -inner_sin]), jnp.stack([inner_sin, inner_cos])]
    )
    inverse_inner = jnp.stack(
        [jnp.stack([inner_cos, inner_sin]), jnp.stack([-inner_sin, inner_cos])]
    )
    return (
        outer_stack,
        inverse_outer,
        jnp.cos(twist_angle)[:, None],
        jnp.sin(twist_angle)[:, None],
        forward_inner,
        inverse_inner,
    )


def forward_transform(signal, tables):
    outer_stack, inverse_outer, twist_re, twist_im, forward_inner, inverse_inner = tables
    first = jnp.einsum(
        "rbkp,cpj->rbckj", outer_stack, signal.astype(jnp.float32), precision=HIGH_PRECISION
    )
    turned = jnp.stack(
        [first[0] * twist_re - first[1] * twist_im, first[0] * twist_im + first[1] * twist_re]
    )
    return jnp.einsum("rsmj,sbckj->rbckm", forward_inner, turned, precision=HIGH_PRECISION)


def inverse_transform(spectrum, tables):
    outer_stack, inverse_outer, twist_re, twist_im, forward_inner, inverse_inner = tables
    back = jnp.einsum("rsjm,sbckm->rbckj", inverse_inner, spectrum, precision=HIGH_PRECISION)
    turned = jnp.stack(
        [back[0] * twist_re + back[1] * twist_im, back[1] * twist_re - back[0] * twist_im]
    )
    return jnp.einsum("rbkp,rbckj->cpj", inverse_outer, turned, precision=HIGH_PRECISION)


def filter_spectrum(residue_local, rate_local, skip_local, devices, rows):
    length = devices * rows
    halves = jnp.arange(2, dtype=jnp.int32)[:, None, None, None]
    coarse = jnp.arange(devices, dtype=jnp.int32)[None, None, :, None]
    fine_pos = jnp.arange(rows, dtype=jnp.int32)[None, None, None, :]
    frequency = 2 * (coarse + devices * fine_pos) + halves
    half_angle = math.pi / (2 * length) * frequency.astype(jnp.float32)
    sine_half = jnp.sin(half_angle)
    sine_sq = sine_half * sine_half
    sine_full = 2.0 * sine_half * jnp.cos(half_angle)
    parity_sign = (1 - 2 * halves).astype(jnp.float32)
    local_width = residue_local.shape[1]
    kernel_re = jnp.zeros((2, local_width, devices, rows), jnp.float32)
    kernel_im = jnp.zeros((2, local_width, devices, rows), jnp.float32)
    for mode_index in range(residue_local.shape[0]):
        rate_row = rate_local[mode_index][None, :, None, None]
        amplitude = residue_local[mode_index][None, :, None, None] * jnp.sqrt(rate_row)
        decay_factor = jnp.exp(-rate_row)
        decay_gap = -jnp.expm1(-rate_row)
        tail_factor = jnp.exp(-rate_row * length)
        denominator = decay_gap * decay_gap + 4.0 * decay_factor * sine_sq
        weighting = amplitude * (1.0 - tail_factor * parity_sign) / denominator
        kernel_re = kernel_re + weighting * (decay_gap + 2.0 * decay_factor * sine_sq)
        kernel_im = kernel_im - weighting * decay_factor * sine_full
    kernel_re = kernel_re + skip_local[None, :, None, None]
    return (kernel_re, kernel_im)


def times_kernel(spectrum, kernel_re, kernel_im):
    return jnp.stack(
        [
            spectrum[0] * kernel_re - spectrum[1] * kernel_im,
            spectrum[0] * kernel_im + spectrum[1] * kernel_re,
        ]
    )


def on_device(proj, short_weight, residues, rates, skip, grad_out):
    devices = lax.axis_size("seq")
    rows = proj.shape[0]
    channels = grad_out.shape[1]
    local_width = channels // devices
    length = devices * rows
    tap_count = short_weight.shape[0]
    first_channel = lax.axis_index("seq") * local_width
    residue_local = lax.dynamic_slice_in_dim(residues, first_channel, local_width, 1)
    rate_local = lax.dynamic_slice_in_dim(rates, first_channel, local_width, 1)
    skip_local = lax.dynamic_slice_in_dim(skip, first_channel, local_width, 0)
    tables = make_tables(devices, rows)
    kernel_re, kernel_im = filter_spectrum(residue_local, rate_local, skip_local, devices, rows)
    arranged = proj.T.reshape(3, devices, local_width, 1, rows)
    streams = lax.all_to_all(arranged, "seq", split_axis=1, concat_axis=3, tiled=True).reshape(
        3, local_width, length
    )
    weight_local = lax.dynamic_slice_in_dim(
        short_weight.reshape(tap_count, 3, channels), first_channel, local_width, 2
    )
    padded = jnp.pad(streams, ((0, 0), (0, 0), (tap_count - 1, 0)))
    filtered = jnp.zeros((3, local_width, length), jnp.float32)
    for tap_index in range(tap_count):
        offset = tap_count - 1 - tap_index
        filtered = filtered + weight_local[tap_index][:, :, None] * padded[
            :, :, offset : offset + length
        ].astype(jnp.float32)
    query_part = filtered[0].reshape(local_width, devices, rows)
    mixed = (filtered[1] * filtered[2]).astype(jnp.bfloat16).reshape(local_width, devices, rows)
    cot_arranged = grad_out.T.reshape(devices, local_width, 1, rows)
    cotangent = lax.all_to_all(
        cot_arranged, "seq", split_axis=0, concat_axis=2, tiled=True
    ).reshape(local_width, devices, rows)
    mixed_spec = forward_transform(mixed, tables)
    conv = inverse_transform(times_kernel(mixed_spec, kernel_re, kernel_im), tables).astype(
        jnp.bfloat16
    )
    gated = (query_part * conv.astype(jnp.float32)).astype(jnp.bfloat16)
    gated_rows = lax.all_to_all(
        gated.reshape(1, local_width, devices, rows), "seq", split_axis=2, concat_axis=0, tiled=True
    )
    gated_output = gated_rows.reshape(channels, rows).T
    scaled = (query_part * cotangent.astype(jnp.float32)).astype(jnp.bfloat16)
    scaled_spec = forward_transform(scaled, tables)
    lag_spec = jnp.stack(
        [
            mixed_spec[0] * scaled_spec[0] + mixed_spec[1] * scaled_spec[1],
            mixed_spec[0] * scaled_spec[1] - mixed_spec[1] * scaled_spec[0],
        ]
    )
    lagged = inverse_transform(lag_spec, tables)
    lagged_rows = lax.all_to_all(
        lagged.reshape(1, local_width, devices, rows),
        "seq",
        split_axis=2,
        concat_axis=0,
        tiled=True,
    )
    filter_grad = lagged_rows.reshape(channels, rows).T
    return (gated_output, filter_grad)


def split_pair(value):
    high = value.astype(jnp.bfloat16)
    low = (value - high.astype(jnp.float32)).astype(jnp.bfloat16)
    return (high, low)


def split_outside(value):
    high = lax.reduce_precision(value, 8, 7)
    return (high.astype(jnp.bfloat16), (value - high).astype(jnp.bfloat16))


def dot32(left, right):
    return jnp.dot(left, right, preferred_element_type=jnp.float32)


def turn(numerator, denominator):
    angle = (2.0 * math.pi / denominator) * (numerator % denominator).astype(jnp.float32)
    return (jnp.cos(angle), jnp.sin(angle))


def spectral_tables(devices, rows, zero):
    fine = FINE_PRODUCT // devices
    coarse = jnp.arange(devices, dtype=jnp.int32) + zero
    place = jnp.arange(rows, dtype=jnp.int32) + zero
    base_cos, base_sin = turn(place[:, None] * place[None, :], rows)
    twist_cos, twist_sin = turn((2 * coarse[:, None] + 1) * place[None, :], 4 * devices * rows)
    cos = base_cos[None] * twist_cos[:, None, :] - base_sin[None] * twist_sin[:, None, :]
    sin = base_sin[None] * twist_cos[:, None, :] + base_cos[None] * twist_sin[:, None, :]
    forward = jnp.concatenate(
        [jnp.concatenate([cos, sin], axis=2), jnp.concatenate([-sin, cos], axis=2)], axis=1
    )
    cos_t = cos.transpose(0, 2, 1)
    sin_t = sin.transpose(0, 2, 1)
    backward = jnp.concatenate(
        [jnp.concatenate([cos_t, -sin_t], axis=2), jnp.concatenate([sin_t, cos_t], axis=2)], axis=1
    )
    outer_cos, outer_sin = turn((2 * coarse[:, None] + 1) * coarse[None, :], 4 * devices)
    eye = jnp.eye(fine, dtype=jnp.float32)
    pair = jnp.stack([outer_cos, -outer_sin], axis=1)
    outer_forward = (pair[:, :, None, :, None] * eye[None, None, :, None, :]).reshape(
        2 * FINE_PRODUCT, FINE_PRODUCT
    )
    back_pair = pair.transpose(2, 0, 1) * (1.0 / (devices * rows))
    outer_backward = (back_pair[:, None, :, :, None] * eye[None, :, None, None, :]).reshape(
        FINE_PRODUCT, 2 * FINE_PRODUCT
    )
    return tuple(
        jnp.concatenate(split_outside(table), axis=-2)
        for table in (forward, backward, outer_forward, outer_backward)
    )


def mix_body(where, query_in, key_in, value_in, before_q, before_k, before_v, weight_q, weight_k, weight_v, cot, sent, query_out, mixed_out, padded):
    taps = weight_q.shape[0]
    rows = query_in.shape[0]
    tail = before_q.shape[0]
    chip, core = where[0], where[1]
    streams = ((query_in, before_q, weight_q), (key_in, before_k, weight_k), (value_in, before_v, weight_v))
    for index, (block, before, _) in enumerate(streams):
        padded[index, :tail, :] = before[...].astype(jnp.float32)
        padded[index, tail:, :] = block[...].astype(jnp.float32)
    for piece in range(query_in.shape[1] // LANES):
        lanes = slice(piece * LANES, (piece + 1) * LANES)
        filtered = []
        for index, (_, _, weight) in enumerate(streams):
            total = None
            for tap in range(taps):
                term = weight[tap : tap + 1, lanes] * padded[index, tail - tap : tail - tap + rows, lanes]
                total = term if total is None else total + term
            filtered.append(total)
        mixed = (filtered[1] * filtered[2]).astype(jnp.bfloat16)
        scaled = (filtered[0] * cot[:, lanes].astype(jnp.float32)).astype(jnp.bfloat16)
        query_out[:, lanes] = filtered[0]
        mixed_out[:, lanes] = mixed
        side = (piece % 2) ^ core
        slot = (piece // 2) ^ (chip % 2)
        sent[side, slot, :, :LANES] = mixed
        sent[side, slot, :, LANES:] = scaled


def mix_streams(where, proj, before, short_weight, grad_out, chunk, chunks, devices):
    rows, channels = grad_out.shape
    taps = short_weight.shape[0]
    tail = before.shape[0]
    chips = devices // 2
    step = 4 * LANES
    steps = channels // chunks // step
    base = chunk * steps
    stride = channels // step

    def stream_spec(height, stream):
        return pl.BlockSpec((height, step), lambda g, w, s=stream: (0, s * stride + base + g))

    return pl.pallas_call(
        mix_body,
        grid_spec=pltpu.PrefetchScalarGridSpec(
            num_scalar_prefetch=1,
            grid=(steps,),
            in_specs=[stream_spec(rows, s) for s in range(3)]
            + [stream_spec(tail, s) for s in range(3)]
            + [stream_spec(taps, s) for s in range(3)]
            + [pl.BlockSpec((rows, step), lambda g, w: (0, base + g))],
            out_specs=[
                pl.BlockSpec((2, 2, rows, 2 * LANES), lambda g, w: (0, g ^ (w[0] // 2), 0, 0)),
                pl.BlockSpec((rows, step), lambda g, w: (0, g)),
                pl.BlockSpec((rows, step), lambda g, w: (0, g)),
            ],
            scratch_shapes=[pltpu.VMEM((3, tail + rows, step), jnp.float32)],
        ),
        out_shape=[
            jax.ShapeDtypeStruct((2, chips, rows, 2 * LANES), jnp.bfloat16),
            jax.ShapeDtypeStruct((rows, channels // chunks), jnp.float32),
            jax.ShapeDtypeStruct((rows, channels // chunks), jnp.bfloat16),
        ],
        cost_estimate=pl.CostEstimate(
            flops=3_000_000, transcendentals=0, bytes_accessed=5_000_000
        ),
        name="mix",
    )(where, *[proj] * 3, *[before] * 3, *[short_weight] * 3, grad_out)


def near_body(mixed, decay, gain, skip, near_out, spread, answer):
    rows, width = mixed.shape
    tiles = width // LANES
    modes = decay.shape[0]
    lines = rows * tiles
    for piece in range(tiles):
        lanes = slice(piece * LANES, (piece + 1) * LANES)
        block = mixed[:, lanes].astype(jnp.float32)
        spread[pl.ds(piece, rows, stride=tiles), :] = block
    for group in range(tiles // 8):
        part = slice(group * 8, group * 8 + 8)
        decays = [decay[r, part, :] for r in range(modes)]
        gains = [gain[r, part, :] for r in range(modes)]
        direct = skip[part, :]

        def step(t, states, group=group, decays=decays, gains=gains, direct=direct):
            at = pl.ds(pl.multiple_of(t * tiles + group * 8, 8), 8)
            here = spread[at, :]
            states = [d * h + here for d, h in zip(decays, states)]
            terms = [g * h for g, h in zip(gains, states)] + [direct * here]
            while len(terms) > 1:
                terms = [a + b for a, b in zip(terms[::2], terms[1::2])] + (
                    terms[-1:] if len(terms) % 2 else []
                )
            answer[at, :] = terms[0]
            return states

        start = [jnp.zeros((8, LANES), jnp.float32)] * modes
        lax.fori_loop(0, rows, step, start, unroll=4)
    for piece in range(tiles):
        lanes = slice(piece * LANES, (piece + 1) * LANES)
        near_out[:, lanes] = answer[pl.ds(piece, rows, stride=tiles), :]


def near_part(mixed, decay, gain, skip):
    rows, width = mixed.shape
    tiles = width // LANES
    return pl.pallas_call(
        near_body,
        out_shape=jax.ShapeDtypeStruct((rows, width), jnp.float32),
        scratch_shapes=[
            pltpu.VMEM((rows * tiles, LANES), jnp.float32),
            pltpu.VMEM((rows * tiles, LANES), jnp.float32),
        ],
        cost_estimate=pl.CostEstimate(
            flops=4_000_000, transcendentals=0, bytes_accessed=8_000_000
        ),
        name="near",
    )(mixed, decay, gain, skip)


def lag_body(where, own, other, *rest):
    count = (len(rest) - 14)
    sources = rest[:count]
    (rate, amplitude, forward, backward, outer_forward, outer_backward, out,
     stacked, lined, high, low, back_high, back_low, spare) = rest[count:]
    step = pl.program_id(0)
    chip, core = where[0], where[1]
    chips = count + 1
    devices = 2 * chips
    rows = own.shape[-2]
    fine = FINE_PRODUCT // devices
    groups = rows // fine
    modes = rate.shape[0]

    @pl.when(step == 0)
    def _():
        for turned in range(chips):
            for side in range(2):
                position = 2 * (turned ^ chip) + (side ^ core)
                at = pl.ds(pl.multiple_of(position * fine, fine), fine)
                if turned == 0:
                    block = (own, other)[side]
                    whole = block[0, 0]
                else:
                    whole = sources[turned - 1][side]
                for group in range(groups):
                    stacked[group, at, :] = whole[group * fine : (group + 1) * fine, :]
                lined[position] = whole[:, :LANES].astype(jnp.float32)
        for group in range(groups):
            signal = stacked[group]
            first = dot32(outer_forward[: 2 * FINE_PRODUCT, :], signal) + dot32(
                outer_forward[2 * FINE_PRODUCT :, :], signal
            )
            first_high, first_low = split_pair(first)
            for k in range(devices):
                for part in range(2):
                    source = slice((2 * k + part) * fine, (2 * k + part + 1) * fine)
                    target = slice(part * rows + group * fine, part * rows + (group + 1) * fine)
                    high[k, target, :] = first_high[source, :]
                    low[k, target, :] = first_low[source, :]

    def inner():
        table = forward[0]
        spectrum = (
            dot32(table[: 2 * rows], high[step])
            + dot32(table[: 2 * rows], low[step])
            + dot32(table[2 * rows :], high[step])
        )
        real_m, imag_m = spectrum[:rows, :LANES], spectrum[rows:, :LANES]
        real_s, imag_s = spectrum[:rows, LANES:], spectrum[rows:, LANES:]
        product = jnp.concatenate(
            [real_m * real_s + imag_m * imag_s, real_m * imag_s - imag_m * real_s], axis=0
        )
        prod_high, prod_low = split_pair(product)
        table_back = backward[0]
        lagged = (
            dot32(table_back[: 2 * rows], prod_high)
            + dot32(table_back[: 2 * rows], prod_low)
            + dot32(table_back[2 * rows :], prod_high)
        )
        lag_high, lag_low = split_pair(lagged)
        for group in range(groups):
            for part in range(2):
                source = slice(part * rows + group * fine, part * rows + (group + 1) * fine)
                at = pl.ds(pl.multiple_of((2 * step + part) * fine, fine), fine)
                back_high[group, at, :] = lag_high[source, :]
                back_low[group, at, :] = lag_low[source, :]

    inner()

    @pl.when(step == 1)
    def _():
        decay = jnp.exp(-rate[...])

        def advance(t, states):
            result = []
            for p in range(devices):
                here = jnp.broadcast_to(lined[p, pl.ds(t, 1), :], (modes, LANES))
                result.append(decay * states[p] + here)
            return tuple(result)

        start = tuple(jnp.zeros((modes, LANES), jnp.float32) for _ in range(devices))
        ends = lax.fori_loop(0, rows, advance, start, unroll=2)
        far = jnp.exp(-float(rows) * rate[...])
        lead = amplitude[...] * decay
        carried = jnp.zeros((modes, LANES), jnp.float32)
        for p in range(devices):
            turned = (p // 2) ^ chip
            side = (p % 2) ^ core
            send_high, send_low = split_pair(lead * carried)
            out[side, turned, rows : rows + modes, :] = send_high
            out[side, turned, rows + modes : rows + 2 * modes, :] = send_low
            carried = far * carried + ends[p]

    @pl.when(step == devices - 1)
    def _():
        for group in range(groups):
            result = (
                dot32(outer_backward[:FINE_PRODUCT, :], back_high[group])
                + dot32(outer_backward[:FINE_PRODUCT, :], back_low[group])
                + dot32(outer_backward[FINE_PRODUCT:, :], back_high[group])
            ).astype(jnp.bfloat16)
            for p in range(devices):
                turned = (p // 2) ^ chip
                side = (p % 2) ^ core
                out[side, turned, group * fine : (group + 1) * fine, :] = result[
                    p * fine : (p + 1) * fine, :
                ]


def lag_part(where, sent, received, moved, rate, amplitude, tables, devices):
    rows = sent.shape[-2]
    chips = devices // 2
    modes = rate.shape[0]
    fine = FINE_PRODUCT // devices
    groups = rows // fine
    forward, backward, outer_forward, outer_backward = tables
    whole = lambda shape: pl.BlockSpec(shape, lambda k, w: (0,) * len(shape))
    return pl.pallas_call(
        lag_body,
        grid_spec=pltpu.PrefetchScalarGridSpec(
            num_scalar_prefetch=1,
            grid=(devices,),
            in_specs=[
                whole((1, 1, rows, 2 * LANES)),
                whole((1, 1, rows, 2 * LANES)),
            ]
            + [whole((2, rows, 2 * LANES))] * (chips - 1)
            + [
                whole((modes, LANES)),
                whole((modes, LANES)),
                pl.BlockSpec((1, 4 * rows, 2 * rows), lambda k, w: (k, 0, 0)),
                pl.BlockSpec((1, 4 * rows, 2 * rows), lambda k, w: (k, 0, 0)),
                whole(outer_forward.shape),
                whole(outer_backward.shape),
            ],
            out_specs=[whole((2, chips, rows + 2 * modes, LANES))],
            scratch_shapes=[
                pltpu.VMEM((groups, FINE_PRODUCT, 2 * LANES), jnp.bfloat16),
                pltpu.VMEM((devices, rows, LANES), jnp.float32),
                pltpu.VMEM((devices, 2 * rows, 2 * LANES), jnp.bfloat16),
                pltpu.VMEM((devices, 2 * rows, 2 * LANES), jnp.bfloat16),
                pltpu.VMEM((groups, 2 * FINE_PRODUCT, LANES), jnp.bfloat16),
                pltpu.VMEM((groups, 2 * FINE_PRODUCT, LANES), jnp.bfloat16),
                pltpu.VMEM((8, LANES), jnp.float32),
            ],
        ),
        out_shape=[jax.ShapeDtypeStruct((2, chips, rows + 2 * modes, LANES), jnp.bfloat16)],
        cost_estimate=pl.CostEstimate(
            flops=5_000_000_000, transcendentals=0, bytes_accessed=12_000_000
        ),
        name="lags",
    )(where, sent, received, *moved, rate, amplitude, forward, backward, outer_forward, outer_backward)[0]


def finish_body(chips, where, own, other, *rest):
    sources = rest[: chips - 1]
    near, query, decay = rest[chips - 1 : chips + 2]
    gated_out, grad_out = rest[-2:]
    chip, core = where[0], where[1]
    rows = near.shape[0]
    modes = decay.shape[0]
    line = lax.broadcasted_iota(jnp.int32, (8, LANES), 0)
    for turned in range(chips):
        for side in range(2):
            owner = 2 * (turned ^ chip) + (side ^ core)
            at = pl.ds(pl.multiple_of(owner * LANES, LANES), LANES)
            block = (own, other)[side].at[0, 0] if turned == 0 else sources[turned - 1].at[side]
            grad_out[:, at] = block[:rows, :].astype(jnp.float32)
            lead = block[rows : rows + modes, :].astype(jnp.float32) + block[
                rows + modes : rows + 2 * modes, :
            ].astype(jnp.float32)
            total = [near[8 * tile : 8 * tile + 8, at] for tile in range(rows // 8)]
            rate_here = decay[:, at]
            for mode in range(modes):
                d1 = jnp.broadcast_to(rate_here[mode : mode + 1, :], (8, LANES))
                d2 = d1 * d1
                d4 = d2 * d2
                d8 = d4 * d4
                ones = jnp.ones_like(d1)
                power = (
                    jnp.where(line & 1 != 0, d1, ones)
                    * jnp.where(line & 2 != 0, d2, ones)
                    * jnp.where(line & 4 != 0, d4, ones)
                )
                term = power * lead[mode : mode + 1, :]
                for tile in range(rows // 8):
                    total[tile] = total[tile] + term
                    if tile + 1 < rows // 8:
                        term = term * d8
            conv = jnp.concatenate(total, axis=0).astype(jnp.bfloat16)
            gated_out[:, at] = (query[:, at] * conv.astype(jnp.float32)).astype(jnp.bfloat16)


def finish_part(where, back, back_other, moved, near, query, decay, previous, chunk, chunks, devices):
    rows, width = near.shape
    chips = devices // 2
    modes = decay.shape[0]
    height = back.shape[2]
    whole = lambda shape: pl.BlockSpec(shape, lambda g, w: (0,) * len(shape))
    in_specs = (
        [whole((1, 1, height, LANES))] * 2
        + [whole((2, height, LANES))] * (chips - 1)
        + [whole((rows, width)), whole((rows, width)), pl.BlockSpec((modes, width), lambda g, w: (0, chunk))]
    )
    args = [back, back_other, *moved, near, query, decay]
    aliases = {}
    if previous is not None:
        in_specs += [pl.BlockSpec(memory_space=pl.ANY)] * 2
        aliases = {len(args) + 1: 0, len(args) + 2: 1}
        args += list(previous)
    return pl.pallas_call(
        functools.partial(finish_body, chips),
        grid_spec=pltpu.PrefetchScalarGridSpec(
            num_scalar_prefetch=1,
            grid=(1,),
            in_specs=in_specs,
            out_specs=[pl.BlockSpec((rows, width), lambda g, w: (0, chunk))] * 2,
        ),
        out_shape=[
            jax.ShapeDtypeStruct((rows, width * chunks), jnp.bfloat16),
            jax.ShapeDtypeStruct((rows, width * chunks), jnp.float32),
        ],
        input_output_aliases=aliases,
        cost_estimate=pl.CostEstimate(
            flops=4_000_000, transcendentals=0, bytes_accessed=5_000_000
        ),
        name="finish",
    )(where, *args)


def swap(value, mask, devices):
    return lax.ppermute(value, "seq", [(i, i ^ mask) for i in range(devices)])


def exchange(outgoing, devices):
    chips = devices // 2
    received = swap(outgoing[1:2], 1, devices)
    moved = [
        swap(jnp.concatenate([outgoing[0, k : k + 1], received[0, k : k + 1]], axis=0), 2 * k, devices)
        for k in range(1, chips)
    ]
    return (received, moved)


def fast_on_device(proj, short_weight, residues, rates, skip, grad_out):
    devices = lax.axis_size("seq")
    rows, channels = grad_out.shape
    modes = rates.shape[0]
    chunks = channels // (devices * LANES)
    me = lax.axis_index("seq")
    where = jnp.stack([me // 2, me % 2]).astype(jnp.int32)
    before = lax.ppermute(
        proj[rows - HALO :], "seq", [(i, i + 1) for i in range(devices - 1)]
    )
    mixes = [
        mix_streams(where, proj, before, short_weight, grad_out, chunk, chunks, devices)
        for chunk in range(chunks)
    ]
    zero = lax.optimization_barrier((jnp.zeros((), jnp.int32), mixes[0][0]))[0]
    tables = spectral_tables(devices, rows, zero)
    decay = jnp.exp(-rates)
    amplitude = residues * jnp.sqrt(rates)
    width = channels // chunks
    backs = []
    for chunk in range(chunks):
        sent, query, mixed = mixes[chunk]
        received, moved = exchange(sent, devices)
        start = chunk * width + me * LANES
        rate_local = lax.dynamic_slice_in_dim(rates, start, LANES, 1)
        amplitude_local = lax.dynamic_slice_in_dim(amplitude, start, LANES, 1)
        backs.append(
            lag_part(where, sent, received, moved, rate_local, amplitude_local, tables, devices)
        )
    shape = (modes, chunks, width // LANES, LANES)
    decay_tiles = decay.reshape(shape)
    gain_tiles = amplitude.reshape(shape)
    skip_tiles = skip.reshape(shape[1:])
    result = None
    for chunk in range(chunks):
        sent, query, mixed = mixes[chunk]
        near = near_part(mixed, decay_tiles[:, chunk], gain_tiles[:, chunk], skip_tiles[chunk])
        received, moved = exchange(backs[chunk], devices)
        result = finish_part(
            where, backs[chunk], received, moved, near, query, decay, result, chunk, chunks, devices
        )
    return tuple(result)


def solution(mesh):
    def body(proj, short_weight, residues, rates, skip, grad_out):
        devices = lax.axis_size("seq")
        rows, channels = grad_out.shape
        fits = (
            devices in (4, 8, 16)
            and rows % LANES == 0
            and channels % (devices * LANES) == 0
            and residues.shape[0] == 16
            and short_weight.shape[0] <= HALO + 1
        )
        chosen = fast_on_device if fits else on_device
        return chosen(proj, short_weight, residues, rates, skip, grad_out)

    return jax.shard_map(
        body,
        mesh=mesh,
        in_specs=(P(("groups", "seq"), None), P(), P(), P(), P(), P(("groups", "seq"), None)),
        out_specs=(P(("groups", "seq"), None), P(("groups", "seq"), None)),
        check_vma=False,
    )
```

```python
import functools
import math

import jax
import jax.numpy as jnp
from jax import lax
from jax.experimental import pallas as pl
from jax.experimental.pallas import tpu as pltpu
from jax.sharding import PartitionSpec as P

HIGH_PRECISION = lax.Precision.HIGH
LANES = 128
HALO = 8
FINE_PRODUCT = 256
UNROLL = 8
CHIP_GROUP = 4
FINISH_GROUP = 4
CHIP_ORDER = (4, 1, 5, 2, 6, 3, 7)
SINE = (1.0, -1.0 / 6, 1.0 / 120, -1.0 / 5040, 1.0 / 362880, -1.0 / 39916800, 1.0 / 6227020800)


def make_tables(devices, rows):
    length = devices * rows
    halves = jnp.arange(2, dtype=jnp.int32)
    coarse = jnp.arange(devices, dtype=jnp.int32)
    fine_pos = jnp.arange(rows, dtype=jnp.int32)
    outer_turn = (
        coarse[None, None, :] * (2 * coarse[None, :, None] + halves[:, None, None]) % (2 * devices)
    )
    outer_angle = -math.pi / devices * outer_turn.astype(jnp.float32)
    twist_turn = (
        fine_pos[None, None, :] * (2 * coarse[None, :, None] + halves[:, None, None]) % (2 * length)
    )
    twist_angle = -math.pi / length * twist_turn.astype(jnp.float32)
    inner_turn = fine_pos[:, None] * fine_pos[None, :] % rows
    inner_angle = -2.0 * math.pi / rows * inner_turn.astype(jnp.float32)
    outer_stack = jnp.stack([jnp.cos(outer_angle), jnp.sin(outer_angle)])
    inverse_outer = outer_stack * (0.5 / length)
    inner_cos = jnp.cos(inner_angle)
    inner_sin = jnp.sin(inner_angle)
    forward_inner = jnp.stack(
        [jnp.stack([inner_cos, -inner_sin]), jnp.stack([inner_sin, inner_cos])]
    )
    inverse_inner = jnp.stack(
        [jnp.stack([inner_cos, inner_sin]), jnp.stack([-inner_sin, inner_cos])]
    )
    return (
        outer_stack,
        inverse_outer,
        jnp.cos(twist_angle)[:, None],
        jnp.sin(twist_angle)[:, None],
        forward_inner,
        inverse_inner,
    )


def forward_transform(signal, tables):
    outer_stack, inverse_outer, twist_re, twist_im, forward_inner, inverse_inner = tables
    first = jnp.einsum(
        "rbkp,cpj->rbckj", outer_stack, signal.astype(jnp.float32), precision=HIGH_PRECISION
    )
    turned = jnp.stack(
        [first[0] * twist_re - first[1] * twist_im, first[0] * twist_im + first[1] * twist_re]
    )
    return jnp.einsum("rsmj,sbckj->rbckm", forward_inner, turned, precision=HIGH_PRECISION)


def inverse_transform(spectrum, tables):
    outer_stack, inverse_outer, twist_re, twist_im, forward_inner, inverse_inner = tables
    back = jnp.einsum("rsjm,sbckm->rbckj", inverse_inner, spectrum, precision=HIGH_PRECISION)
    turned = jnp.stack(
        [back[0] * twist_re + back[1] * twist_im, back[1] * twist_re - back[0] * twist_im]
    )
    return jnp.einsum("rbkp,rbckj->cpj", inverse_outer, turned, precision=HIGH_PRECISION)


def filter_spectrum(residue_local, rate_local, skip_local, devices, rows):
    length = devices * rows
    halves = jnp.arange(2, dtype=jnp.int32)[:, None, None, None]
    coarse = jnp.arange(devices, dtype=jnp.int32)[None, None, :, None]
    fine_pos = jnp.arange(rows, dtype=jnp.int32)[None, None, None, :]
    frequency = 2 * (coarse + devices * fine_pos) + halves
    half_angle = math.pi / (2 * length) * frequency.astype(jnp.float32)
    sine_half = jnp.sin(half_angle)
    sine_sq = sine_half * sine_half
    sine_full = 2.0 * sine_half * jnp.cos(half_angle)
    parity_sign = (1 - 2 * halves).astype(jnp.float32)
    local_width = residue_local.shape[1]
    kernel_re = jnp.zeros((2, local_width, devices, rows), jnp.float32)
    kernel_im = jnp.zeros((2, local_width, devices, rows), jnp.float32)
    for mode_index in range(residue_local.shape[0]):
        rate_row = rate_local[mode_index][None, :, None, None]
        amplitude = residue_local[mode_index][None, :, None, None] * jnp.sqrt(rate_row)
        decay_factor = jnp.exp(-rate_row)
        decay_gap = -jnp.expm1(-rate_row)
        tail_factor = jnp.exp(-rate_row * length)
        denominator = decay_gap * decay_gap + 4.0 * decay_factor * sine_sq
        weighting = amplitude * (1.0 - tail_factor * parity_sign) / denominator
        kernel_re = kernel_re + weighting * (decay_gap + 2.0 * decay_factor * sine_sq)
        kernel_im = kernel_im - weighting * decay_factor * sine_full
    kernel_re = kernel_re + skip_local[None, :, None, None]
    return (kernel_re, kernel_im)


def times_kernel(spectrum, kernel_re, kernel_im):
    return jnp.stack(
        [
            spectrum[0] * kernel_re - spectrum[1] * kernel_im,
            spectrum[0] * kernel_im + spectrum[1] * kernel_re,
        ]
    )


def on_device(proj, short_weight, residues, rates, skip, grad_out):
    devices = lax.axis_size("seq")
    rows = proj.shape[0]
    channels = grad_out.shape[1]
    local_width = channels // devices
    length = devices * rows
    tap_count = short_weight.shape[0]
    first_channel = lax.axis_index("seq") * local_width
    residue_local = lax.dynamic_slice_in_dim(residues, first_channel, local_width, 1)
    rate_local = lax.dynamic_slice_in_dim(rates, first_channel, local_width, 1)
    skip_local = lax.dynamic_slice_in_dim(skip, first_channel, local_width, 0)
    tables = make_tables(devices, rows)
    kernel_re, kernel_im = filter_spectrum(residue_local, rate_local, skip_local, devices, rows)
    arranged = proj.T.reshape(3, devices, local_width, 1, rows)
    streams = lax.all_to_all(arranged, "seq", split_axis=1, concat_axis=3, tiled=True).reshape(
        3, local_width, length
    )
    weight_local = lax.dynamic_slice_in_dim(
        short_weight.reshape(tap_count, 3, channels), first_channel, local_width, 2
    )
    padded = jnp.pad(streams, ((0, 0), (0, 0), (tap_count - 1, 0)))
    filtered = jnp.zeros((3, local_width, length), jnp.float32)
    for tap_index in range(tap_count):
        offset = tap_count - 1 - tap_index
        filtered = filtered + weight_local[tap_index][:, :, None] * padded[
            :, :, offset : offset + length
        ].astype(jnp.float32)
    query_part = filtered[0].reshape(local_width, devices, rows)
    mixed = (filtered[1] * filtered[2]).astype(jnp.bfloat16).reshape(local_width, devices, rows)
    cot_arranged = grad_out.T.reshape(devices, local_width, 1, rows)
    cotangent = lax.all_to_all(
        cot_arranged, "seq", split_axis=0, concat_axis=2, tiled=True
    ).reshape(local_width, devices, rows)
    mixed_spec = forward_transform(mixed, tables)
    conv = inverse_transform(times_kernel(mixed_spec, kernel_re, kernel_im), tables).astype(
        jnp.bfloat16
    )
    gated = (query_part * conv.astype(jnp.float32)).astype(jnp.bfloat16)
    gated_rows = lax.all_to_all(
        gated.reshape(1, local_width, devices, rows), "seq", split_axis=2, concat_axis=0, tiled=True
    )
    gated_output = gated_rows.reshape(channels, rows).T
    scaled = (query_part * cotangent.astype(jnp.float32)).astype(jnp.bfloat16)
    scaled_spec = forward_transform(scaled, tables)
    lag_spec = jnp.stack(
        [
            mixed_spec[0] * scaled_spec[0] + mixed_spec[1] * scaled_spec[1],
            mixed_spec[0] * scaled_spec[1] - mixed_spec[1] * scaled_spec[0],
        ]
    )
    lagged = inverse_transform(lag_spec, tables)
    lagged_rows = lax.all_to_all(
        lagged.reshape(1, local_width, devices, rows),
        "seq",
        split_axis=2,
        concat_axis=0,
        tiled=True,
    )
    filter_grad = lagged_rows.reshape(channels, rows).T
    return (gated_output, filter_grad)


def split_pair(value):
    high = value.astype(jnp.bfloat16)
    low = (value - high.astype(jnp.float32)).astype(jnp.bfloat16)
    return (high, low)


def split_outside(value):
    high = lax.reduce_precision(value, 8, 7)
    return (high.astype(jnp.bfloat16), (value - high).astype(jnp.bfloat16))


def dot32(left, right):
    return jnp.dot(left, right, preferred_element_type=jnp.float32)


def cosines(turns, whole):
    folded = jnp.bitwise_and(turns + whole // 2, whole - 1) - whole // 2
    angle = (2.0 * math.pi / whole) * (whole // 4 - jnp.abs(folded)).astype(jnp.float32)
    square = angle * angle
    series = jnp.full_like(angle, SINE[-1])
    for factor in SINE[-2::-1]:
        series = series * square + factor
    return angle * series


def grid_of(height, width, zero):
    shape = (height, width)
    return (
        lax.broadcasted_iota(jnp.int32, shape, 0) + zero,
        lax.broadcasted_iota(jnp.int32, shape, 1) + zero,
    )


def spectral_tables(devices, rows, zero):
    fine = FINE_PRODUCT // devices
    line, lane = grid_of(2 * rows, 2 * rows, zero)
    quarter = (line // rows - lane // rows) * (rows // 4)
    base = cosines((line % rows) * (lane % rows) + quarter, rows)
    base_back = cosines((line % rows) * (lane % rows) - quarter, rows)
    line, lane = grid_of(2 * FINE_PRODUCT, FINE_PRODUCT, zero)
    coarse = line % FINE_PRODUCT // fine
    outer = jnp.where(
        line % fine == lane % fine,
        cosines((2 * coarse + 1) * (lane // fine) + line // FINE_PRODUCT * devices, 4 * devices),
        0.0,
    )
    line, lane = grid_of(FINE_PRODUCT, 2 * FINE_PRODUCT, zero)
    coarse = lane % FINE_PRODUCT // fine
    outer_back = jnp.where(
        line % fine == lane % fine,
        cosines((2 * coarse + 1) * (line // fine) + lane // FINE_PRODUCT * devices, 4 * devices)
        * (1.0 / (devices * rows)),
        0.0,
    )
    line, lane = grid_of(FINE_PRODUCT, LANES, zero)
    odd = 2 * (line // fine) + 1
    length = devices * rows
    first = odd * (line % fine)
    twist = jnp.stack(
        [
            cosines(first, 4 * length),
            cosines(first - length, 4 * length),
            cosines(odd * fine, 4 * length),
            cosines(odd * fine - length, 4 * length),
        ]
    )
    packed = [
        jnp.concatenate(split_outside(table), axis=0)
        for table in (base, base_back, outer, outer_back)
    ]
    return (*packed, twist)


def mix_body(where, query_in, key_in, value_in, before_q, before_k, before_v, weight_q, weight_k, weight_v, cot, kept, given, query_out, mixed_out, padded):
    taps = weight_q.shape[0]
    rows = query_in.shape[0]
    tail = before_q.shape[0]
    chip, core = where[0], where[1]
    streams = ((query_in, before_q, weight_q), (key_in, before_k, weight_k), (value_in, before_v, weight_v))
    for index, (block, before, _) in enumerate(streams):
        padded[index, :tail, :] = before[...].astype(jnp.float32)
        padded[index, tail:, :] = block[...].astype(jnp.float32)
    group = kept.shape[0]
    for index in range(group):
        slot = index ^ (chip % group)
        for side, sent in enumerate((kept, given)):
            piece = 2 * index + (core ^ side)
            lanes = pl.ds(pl.multiple_of(piece * LANES, LANES), LANES)
            filtered = []
            for stream, (_, _, weight) in enumerate(streams):
                total = None
                for tap in range(taps):
                    term = weight[tap : tap + 1, lanes] * padded[stream, tail - tap : tail - tap + rows, lanes]
                    total = term if total is None else total + term
                filtered.append(total)
            mixed = (filtered[1] * filtered[2]).astype(jnp.bfloat16)
            scaled = (filtered[0] * cot[:, lanes].astype(jnp.float32)).astype(jnp.bfloat16)
            query_out[:, lanes] = filtered[0]
            mixed_out[:, lanes] = mixed
            sent[slot, :, :LANES] = mixed
            sent[slot, :, LANES:] = scaled


def mix_streams(where, proj, before, short_weight, grad_out, chunk, chunks, devices):
    rows, channels = grad_out.shape
    taps = short_weight.shape[0]
    tail = before.shape[0]
    chips = devices // 2
    group = CHIP_GROUP
    step = 2 * group * LANES
    steps = channels // chunks // step
    base = chunk * steps
    stride = channels // step

    def stream_spec(height, stream):
        return pl.BlockSpec((height, step), lambda g, w, s=stream: (0, s * stride + base + g))

    return pl.pallas_call(
        mix_body,
        grid_spec=pltpu.PrefetchScalarGridSpec(
            num_scalar_prefetch=1,
            grid=(steps,),
            in_specs=[stream_spec(rows, s) for s in range(3)]
            + [stream_spec(tail, s) for s in range(3)]
            + [stream_spec(taps, s) for s in range(3)]
            + [pl.BlockSpec((rows, step), lambda g, w: (0, base + g))],
            out_specs=[
                pl.BlockSpec((group, rows, 2 * LANES), lambda g, w: (g ^ (w[0] // group), 0, 0)),
                pl.BlockSpec((group, rows, 2 * LANES), lambda g, w: (g ^ (w[0] // group), 0, 0)),
                pl.BlockSpec((rows, step), lambda g, w: (0, g)),
                pl.BlockSpec((rows, step), lambda g, w: (0, g)),
            ],
            scratch_shapes=[pltpu.VMEM((3, tail + rows, step), jnp.float32)],
        ),
        out_shape=[
            jax.ShapeDtypeStruct((chips, rows, 2 * LANES), jnp.bfloat16),
            jax.ShapeDtypeStruct((chips, rows, 2 * LANES), jnp.bfloat16),
            jax.ShapeDtypeStruct((rows, channels // chunks), jnp.float32),
            jax.ShapeDtypeStruct((rows, channels // chunks), jnp.bfloat16),
        ],
        cost_estimate=pl.CostEstimate(
            flops=3_000_000, transcendentals=0, bytes_accessed=5_000_000
        ),
        name="mix",
    )(where, *[proj] * 3, *[before] * 3, *[short_weight] * 3, grad_out)


def near_body(mixed, decay, gain, skip, near_out, spread, answer):
    rows, width = mixed.shape
    tiles = width // LANES
    modes = decay.shape[0]
    lines = rows * tiles
    for piece in range(tiles):
        lanes = slice(piece * LANES, (piece + 1) * LANES)
        block = mixed[:, lanes].astype(jnp.float32)
        spread[pl.ds(piece, rows, stride=tiles), :] = block
    for group in range(tiles // 8):
        part = slice(group * 8, group * 8 + 8)
        decays = [decay[r, part, :] for r in range(modes)]
        gains = [gain[r, part, :] for r in range(modes)]
        direct = skip[part, :]

        def step(t, states, group=group, decays=decays, gains=gains, direct=direct):
            at = pl.ds(pl.multiple_of(t * tiles + group * 8, 8), 8)
            here = spread[at, :]
            states = [d * h + here for d, h in zip(decays, states)]
            terms = [g * h for g, h in zip(gains, states)] + [direct * here]
            while len(terms) > 1:
                terms = [a + b for a, b in zip(terms[::2], terms[1::2])] + (
                    terms[-1:] if len(terms) % 2 else []
                )
            answer[at, :] = terms[0]
            return states

        start = [jnp.zeros((8, LANES), jnp.float32)] * modes
        lax.fori_loop(0, rows, step, start, unroll=4)
    for piece in range(tiles):
        lanes = slice(piece * LANES, (piece + 1) * LANES)
        near_out[:, lanes] = answer[pl.ds(piece, rows, stride=tiles), :]


def near_part(mixed, decay, gain, skip):
    rows, width = mixed.shape
    tiles = width // LANES
    return pl.pallas_call(
        near_body,
        out_shape=jax.ShapeDtypeStruct((rows, width), jnp.float32),
        scratch_shapes=[
            pltpu.VMEM((rows * tiles, LANES), jnp.float32),
            pltpu.VMEM((rows * tiles, LANES), jnp.float32),
        ],
        cost_estimate=pl.CostEstimate(
            flops=4_000_000, transcendentals=0, bytes_accessed=8_000_000
        ),
        name="near",
    )(mixed, decay, gain, skip)


def lag_body(chips, where, own, other, *rest):
    sources = rest[: chips - 1]
    (rate, amplitude, forward, backward, outer_forward, outer_backward, twist, out,
     stacked, lined, high, low, back, turns) = rest[chips - 1 :]
    chip, core = where[0], where[1]
    devices = 2 * chips
    rows = own.shape[-2]
    fine = FINE_PRODUCT // devices
    groups = rows // fine
    modes = rate.shape[0]

    for turned in range(chips):
        for side in range(2):
            position = 2 * (turned ^ chip) + (side ^ core)
            at = pl.ds(pl.multiple_of(position * fine, fine), fine)
            whole = (own, other)[side][0] if turned == 0 else sources[turned - 1][side]
            for group in range(groups):
                stacked[group, at, :] = whole[group * fine : (group + 1) * fine, :]
            lined[position] = whole[:, :LANES].astype(jnp.float32)

    turns[0, 0] = twist[0]
    turns[0, 1] = twist[1]
    for group in range(1, groups):
        cos, sin = turns[group - 1, 0], turns[group - 1, 1]
        turns[group, 0] = cos * twist[2] - sin * twist[3]
        turns[group, 1] = sin * twist[2] + cos * twist[3]

    def outer_step(group, carry):
        signal = stacked[group]
        first = dot32(outer_forward[: 2 * FINE_PRODUCT, :], signal) + dot32(
            outer_forward[2 * FINE_PRODUCT :, :], signal
        )
        cos, sin = turns[group, 0], turns[group, 1]
        cos = jnp.concatenate([cos, cos], axis=1)
        sin = jnp.concatenate([sin, sin], axis=1)
        real, imag = first[:FINE_PRODUCT], first[FINE_PRODUCT:]
        pairs = (split_pair(real * cos + imag * sin), split_pair(imag * cos - real * sin))
        for k in range(devices):
            source = slice(k * fine, (k + 1) * fine)
            for part in range(2):
                at = pl.ds(pl.multiple_of(part * rows + group * fine, fine), fine)
                high[k, at, :] = pairs[part][0][source, :]
                low[k, at, :] = pairs[part][1][source, :]
        return carry

    lax.fori_loop(0, groups, outer_step, 0, unroll=4)

    def inner_step(k, carry):
        spectrum = (
            dot32(forward[: 2 * rows], high[k])
            + dot32(forward[: 2 * rows], low[k])
            + dot32(forward[2 * rows :], high[k])
        )
        real_m, imag_m = spectrum[:rows, :LANES], spectrum[rows:, :LANES]
        real_s, imag_s = spectrum[:rows, LANES:], spectrum[rows:, LANES:]
        product = jnp.concatenate(
            [real_m * real_s + imag_m * imag_s, real_m * imag_s - imag_m * real_s], axis=0
        )
        prod_high, prod_low = split_pair(product)
        lagged = (
            dot32(backward[: 2 * rows], prod_high)
            + dot32(backward[: 2 * rows], prod_low)
            + dot32(backward[2 * rows :], prod_high)
        )
        for group in range(groups):
            for part in range(2):
                source = slice(part * rows + group * fine, part * rows + (group + 1) * fine)
                at = pl.ds(pl.multiple_of(part * FINE_PRODUCT + k * fine, fine), fine)
                back[group, at, :] = lagged[source, :]
        return carry

    lax.fori_loop(0, devices, inner_step, 0, unroll=UNROLL)

    decay = jnp.exp(-rate[...])

    def advance(t, states):
        result = []
        for p in range(devices):
            here = jnp.broadcast_to(lined[p, pl.ds(t, 1), :], (modes, LANES))
            result.append(decay * states[p] + here)
        return tuple(result)

    start = tuple(jnp.zeros((modes, LANES), jnp.float32) for _ in range(devices))
    ends = lax.fori_loop(0, rows, advance, start, unroll=8)
    far = jnp.exp(-float(rows) * rate[...])
    lead = amplitude[...] * decay
    carried = jnp.zeros((modes, LANES), jnp.float32)
    for p in range(devices):
        turned = (p // 2) ^ chip
        side = (p % 2) ^ core
        send_high, send_low = split_pair(lead * carried)
        out[side, turned, rows : rows + modes, :] = send_high
        out[side, turned, rows + modes : rows + 2 * modes, :] = send_low
        carried = far * carried + ends[p]

    def last_step(group, carry):
        cos, sin = turns[group, 0], turns[group, 1]
        real, imag = back[group, :FINE_PRODUCT, :], back[group, FINE_PRODUCT:, :]
        turned_back = jnp.concatenate([real * cos - imag * sin, real * sin + imag * cos], axis=0)
        back_high, back_low = split_pair(turned_back)
        result = (
            dot32(outer_backward[:FINE_PRODUCT, :], back_high)
            + dot32(outer_backward[:FINE_PRODUCT, :], back_low)
            + dot32(outer_backward[FINE_PRODUCT:, :], back_high)
        ).astype(jnp.bfloat16)
        at = pl.ds(pl.multiple_of(group * fine, fine), fine)
        for p in range(devices):
            turned = (p // 2) ^ chip
            side = (p % 2) ^ core
            out[side, turned, at, :] = result[p * fine : (p + 1) * fine, :]
        return carry

    lax.fori_loop(0, groups, last_step, 0, unroll=4)


def lag_part(where, sent, received, moved, rate, amplitude, tables, devices):
    rows = sent.shape[-2]
    chips = devices // 2
    modes = rate.shape[0]
    groups = rows * devices // FINE_PRODUCT
    whole = lambda shape: pl.BlockSpec(shape, lambda k, w: (0,) * len(shape))
    return pl.pallas_call(
        functools.partial(lag_body, chips),
        grid_spec=pltpu.PrefetchScalarGridSpec(
            num_scalar_prefetch=1,
            grid=(1,),
            in_specs=[whole((1, rows, 2 * LANES))] * 2
            + [whole((2, rows, 2 * LANES))] * (chips - 1)
            + [whole((modes, LANES))] * 2
            + [whole(table.shape) for table in tables],
            out_specs=[whole((2, chips, rows + 2 * modes, LANES))],
            scratch_shapes=[
                pltpu.VMEM((groups, FINE_PRODUCT, 2 * LANES), jnp.bfloat16),
                pltpu.VMEM((devices, rows, LANES), jnp.float32),
                pltpu.VMEM((devices, 2 * rows, 2 * LANES), jnp.bfloat16),
                pltpu.VMEM((devices, 2 * rows, 2 * LANES), jnp.bfloat16),
                pltpu.VMEM((groups, 2 * FINE_PRODUCT, LANES), jnp.float32),
                pltpu.VMEM((groups, 2, FINE_PRODUCT, LANES), jnp.float32),
            ],
        ),
        out_shape=[jax.ShapeDtypeStruct((2, chips, rows + 2 * modes, LANES), jnp.bfloat16)],
        cost_estimate=pl.CostEstimate(
            flops=5_000_000_000, transcendentals=0, bytes_accessed=12_000_000
        ),
        name="lags",
    )(where, sent, received, *moved, rate, amplitude, *tables)[0]


def finish_body(chips, group, where, own, other, *rest):
    sources = rest[: chips - 1]
    near, query, decay = rest[chips - 1 : chips + 2]
    gated_out, grad_out = rest[-2:]
    chip, core = where[0], where[1]
    rows = near.shape[0]
    modes = decay.shape[0]
    line = lax.broadcasted_iota(jnp.int32, (8, LANES), 0)

    def work(turned, side):
        column = 2 * ((turned ^ chip) % group) + (side ^ core)
        at = pl.ds(pl.multiple_of(column * LANES, LANES), LANES)
        block = (own, other)[side].at[0] if turned == 0 else sources[turned - 1].at[side]
        grad_out[:, at] = block[:rows, :].astype(jnp.float32)
        lead = block[rows : rows + modes, :].astype(jnp.float32) + block[
            rows + modes : rows + 2 * modes, :
        ].astype(jnp.float32)
        total = [near[8 * tile : 8 * tile + 8, at] for tile in range(rows // 8)]
        rate_here = decay[:, at]
        for mode in range(modes):
            d1 = jnp.broadcast_to(rate_here[mode : mode + 1, :], (8, LANES))
            d2 = d1 * d1
            d4 = d2 * d2
            d8 = d4 * d4
            ones = jnp.ones_like(d1)
            power = (
                jnp.where(line & 1 != 0, d1, ones)
                * jnp.where(line & 2 != 0, d2, ones)
                * jnp.where(line & 4 != 0, d4, ones)
            )
            term = power * lead[mode : mode + 1, :]
            for tile in range(rows // 8):
                total[tile] = total[tile] + term
                if tile + 1 < rows // 8:
                    term = term * d8
        conv = jnp.concatenate(total, axis=0).astype(jnp.bfloat16)
        gated_out[:, at] = (query[:, at] * conv.astype(jnp.float32)).astype(jnp.bfloat16)

    for first in range(0, chips, group):

        @pl.when(pl.program_id(0) == first // group)
        def _(first=first):
            for turned in range(first, first + group):
                for side in range(2):
                    work(turned, side)


def finish_part(where, back, back_other, moved, near, query, decay, previous, chunk, chunks, devices):
    rows, width = near.shape
    chips = devices // 2
    modes = decay.shape[0]
    height = back.shape[1]
    group = FINISH_GROUP
    step = 2 * group * LANES
    steps = width // step
    whole = lambda shape: pl.BlockSpec(shape, lambda g, w: (0,) * len(shape))
    column = lambda g, w: g ^ (w[0] // group)
    in_specs = (
        [whole((1, height, LANES))] * 2
        + [whole((2, height, LANES))] * (chips - 1)
        + [pl.BlockSpec((rows, step), lambda g, w: (0, column(g, w)))] * 2
        + [pl.BlockSpec((modes, step), lambda g, w: (0, chunk * steps + column(g, w)))]
    )
    args = [back, back_other, *moved, near, query, decay]
    aliases = {}
    if previous is not None:
        in_specs += [pl.BlockSpec(memory_space=pl.ANY)] * 2
        aliases = {len(args) + 1: 0, len(args) + 2: 1}
        args += list(previous)
    return pl.pallas_call(
        functools.partial(finish_body, chips, group),
        grid_spec=pltpu.PrefetchScalarGridSpec(
            num_scalar_prefetch=1,
            grid=(steps,),
            in_specs=in_specs,
            out_specs=[
                pl.BlockSpec((rows, step), lambda g, w: (0, chunk * steps + column(g, w)))
            ]
            * 2,
        ),
        out_shape=[
            jax.ShapeDtypeStruct((rows, width * chunks), jnp.bfloat16),
            jax.ShapeDtypeStruct((rows, width * chunks), jnp.float32),
        ],
        input_output_aliases=aliases,
        cost_estimate=pl.CostEstimate(
            flops=4_000_000, transcendentals=0, bytes_accessed=5_000_000
        ),
        name="finish",
    )(where, *args)


def swap(value, mask, devices):
    return lax.ppermute(value, "seq", [(i, i ^ mask) for i in range(devices)])


def after(value, *earlier):
    return lax.optimization_barrier((value, earlier))[0]


def hand_over(given, devices):
    return swap(given, 1, devices)


def spread_out(kept, received, devices):
    chips = devices // 2
    moved = {}
    for k in CHIP_ORDER:
        if k < chips:
            block = jnp.concatenate([kept[k : k + 1], received[k : k + 1]], axis=0)
            moved[k] = swap(block, 2 * k, devices)
    return [moved[k] for k in range(1, chips)]


def fast_on_device(proj, short_weight, residues, rates, skip, grad_out):
    devices = lax.axis_size("seq")
    rows, channels = grad_out.shape
    modes = rates.shape[0]
    chunks = channels // (devices * LANES)
    width = channels // chunks
    me = lax.axis_index("seq")
    where = jnp.stack([me // 2, me % 2]).astype(jnp.int32)
    before = lax.ppermute(
        proj[rows - HALO :], "seq", [(i, i + 1) for i in range(devices - 1)]
    )
    shape = (modes, chunks, width // LANES, LANES)
    mixes, ready = [], []
    token = before
    for chunk in range(chunks):
        kept, given, query, mixed = mix_streams(
            after(where, token), proj, before, short_weight, grad_out, chunk, chunks, devices
        )
        received = hand_over(given, devices)
        moved = spread_out(kept, received, devices)
        mixes.append((query, mixed))
        ready.append((kept, received, moved))
        token = moved[0]
    last = ready[-1][1]
    zero = after(jnp.zeros((), jnp.int32), last)
    tables = spectral_tables(devices, rows, zero)
    rates_late, residues_late, skip_late = after((rates, residues, skip), last)
    decay = jnp.exp(-rates_late)
    amplitude = residues_late * jnp.sqrt(rates_late)
    decay_tiles = decay.reshape(shape)
    gain_tiles = amplitude.reshape(shape)
    skip_tiles = skip_late.reshape(shape[1:])
    result = None
    nears, returns = [], []
    token = None
    for chunk in range(chunks):
        kept, received, moved = ready[chunk]
        near = near_part(
            after(mixes[chunk][1], tables if token is None else token),
            decay_tiles[:, chunk],
            gain_tiles[:, chunk],
            skip_tiles[chunk],
        )
        start = chunk * width + me * LANES
        rate_local = lax.dynamic_slice_in_dim(rates_late, start, LANES, 1)
        amplitude_local = lax.dynamic_slice_in_dim(amplitude, start, LANES, 1)
        guard = (token,) if chunk else (near, *[one[2][0] for one in ready[1:2]])
        back = lag_part(
            after(where, *guard), kept, received, moved, rate_local, amplitude_local, tables, devices
        )
        back_received = hand_over(back[1], devices)
        back_moved = spread_out(back[0], back_received, devices)
        nears.append(near)
        returns.append((back[0], back_received, back_moved))
        token = back_moved[0]
    for chunk in range(chunks):
        back_kept, back_received, back_moved = returns[chunk]
        result = finish_part(
            where, back_kept, back_received, back_moved, nears[chunk], mixes[chunk][0], decay,
            result, chunk, chunks, devices,
        )
    return tuple(result)


def solution(mesh):
    def body(proj, short_weight, residues, rates, skip, grad_out):
        devices = lax.axis_size("seq")
        rows, channels = grad_out.shape
        fits = (
            devices in (4, 8, 16)
            and rows % LANES == 0
            and channels % (devices * LANES) == 0
            and residues.shape[0] == 16
            and short_weight.shape[0] <= HALO + 1
        )
        chosen = fast_on_device if fits else on_device
        return chosen(proj, short_weight, residues, rates, skip, grad_out)

    return jax.shard_map(
        body,
        mesh=mesh,
        in_specs=(P(("groups", "seq"), None), P(), P(), P(), P(), P(("groups", "seq"), None)),
        out_specs=(P(("groups", "seq"), None), P(("groups", "seq"), None)),
        check_vma=False,
    )
```

```python
import functools
import math

import jax
import jax.numpy as jnp
from jax import lax
from jax.experimental import pallas as pl
from jax.experimental.pallas import tpu as pltpu
from jax.sharding import PartitionSpec as P

HIGH_PRECISION = lax.Precision.HIGH
LANES = 128
HALO = 8
FINE_PRODUCT = 256
UNROLL = 8
STRIP = 32
PLANE = 4
PAIR = 2
SINE = (1.0, -1.0 / 6, 1.0 / 120, -1.0 / 5040, 1.0 / 362880, -1.0 / 39916800, 1.0 / 6227020800)


def make_tables(devices, rows):
    length = devices * rows
    halves = jnp.arange(2, dtype=jnp.int32)
    coarse = jnp.arange(devices, dtype=jnp.int32)
    fine_pos = jnp.arange(rows, dtype=jnp.int32)
    outer_turn = (
        coarse[None, None, :] * (2 * coarse[None, :, None] + halves[:, None, None]) % (2 * devices)
    )
    outer_angle = -math.pi / devices * outer_turn.astype(jnp.float32)
    twist_turn = (
        fine_pos[None, None, :] * (2 * coarse[None, :, None] + halves[:, None, None]) % (2 * length)
    )
    twist_angle = -math.pi / length * twist_turn.astype(jnp.float32)
    inner_turn = fine_pos[:, None] * fine_pos[None, :] % rows
    inner_angle = -2.0 * math.pi / rows * inner_turn.astype(jnp.float32)
    outer_stack = jnp.stack([jnp.cos(outer_angle), jnp.sin(outer_angle)])
    inverse_outer = outer_stack * (0.5 / length)
    inner_cos = jnp.cos(inner_angle)
    inner_sin = jnp.sin(inner_angle)
    forward_inner = jnp.stack(
        [jnp.stack([inner_cos, -inner_sin]), jnp.stack([inner_sin, inner_cos])]
    )
    inverse_inner = jnp.stack(
        [jnp.stack([inner_cos, inner_sin]), jnp.stack([-inner_sin, inner_cos])]
    )
    return (
        outer_stack,
        inverse_outer,
        jnp.cos(twist_angle)[:, None],
        jnp.sin(twist_angle)[:, None],
        forward_inner,
        inverse_inner,
    )


def forward_transform(signal, tables):
    outer_stack, inverse_outer, twist_re, twist_im, forward_inner, inverse_inner = tables
    first = jnp.einsum(
        "rbkp,cpj->rbckj", outer_stack, signal.astype(jnp.float32), precision=HIGH_PRECISION
    )
    turned = jnp.stack(
        [first[0] * twist_re - first[1] * twist_im, first[0] * twist_im + first[1] * twist_re]
    )
    return jnp.einsum("rsmj,sbckj->rbckm", forward_inner, turned, precision=HIGH_PRECISION)


def inverse_transform(spectrum, tables):
    outer_stack, inverse_outer, twist_re, twist_im, forward_inner, inverse_inner = tables
    back = jnp.einsum("rsjm,sbckm->rbckj", inverse_inner, spectrum, precision=HIGH_PRECISION)
    turned = jnp.stack(
        [back[0] * twist_re + back[1] * twist_im, back[1] * twist_re - back[0] * twist_im]
    )
    return jnp.einsum("rbkp,rbckj->cpj", inverse_outer, turned, precision=HIGH_PRECISION)


def filter_spectrum(residue_local, rate_local, skip_local, devices, rows):
    length = devices * rows
    halves = jnp.arange(2, dtype=jnp.int32)[:, None, None, None]
    coarse = jnp.arange(devices, dtype=jnp.int32)[None, None, :, None]
    fine_pos = jnp.arange(rows, dtype=jnp.int32)[None, None, None, :]
    frequency = 2 * (coarse + devices * fine_pos) + halves
    half_angle = math.pi / (2 * length) * frequency.astype(jnp.float32)
    sine_half = jnp.sin(half_angle)
    sine_sq = sine_half * sine_half
    sine_full = 2.0 * sine_half * jnp.cos(half_angle)
    parity_sign = (1 - 2 * halves).astype(jnp.float32)
    local_width = residue_local.shape[1]
    kernel_re = jnp.zeros((2, local_width, devices, rows), jnp.float32)
    kernel_im = jnp.zeros((2, local_width, devices, rows), jnp.float32)
    for mode_index in range(residue_local.shape[0]):
        rate_row = rate_local[mode_index][None, :, None, None]
        amplitude = residue_local[mode_index][None, :, None, None] * jnp.sqrt(rate_row)
        decay_factor = jnp.exp(-rate_row)
        decay_gap = -jnp.expm1(-rate_row)
        tail_factor = jnp.exp(-rate_row * length)
        denominator = decay_gap * decay_gap + 4.0 * decay_factor * sine_sq
        weighting = amplitude * (1.0 - tail_factor * parity_sign) / denominator
        kernel_re = kernel_re + weighting * (decay_gap + 2.0 * decay_factor * sine_sq)
        kernel_im = kernel_im - weighting * decay_factor * sine_full
    kernel_re = kernel_re + skip_local[None, :, None, None]
    return (kernel_re, kernel_im)


def times_kernel(spectrum, kernel_re, kernel_im):
    return jnp.stack(
        [
            spectrum[0] * kernel_re - spectrum[1] * kernel_im,
            spectrum[0] * kernel_im + spectrum[1] * kernel_re,
        ]
    )


def on_device(proj, short_weight, residues, rates, skip, grad_out):
    devices = lax.axis_size("seq")
    rows = proj.shape[0]
    channels = grad_out.shape[1]
    local_width = channels // devices
    length = devices * rows
    tap_count = short_weight.shape[0]
    first_channel = lax.axis_index("seq") * local_width
    residue_local = lax.dynamic_slice_in_dim(residues, first_channel, local_width, 1)
    rate_local = lax.dynamic_slice_in_dim(rates, first_channel, local_width, 1)
    skip_local = lax.dynamic_slice_in_dim(skip, first_channel, local_width, 0)
    tables = make_tables(devices, rows)
    kernel_re, kernel_im = filter_spectrum(residue_local, rate_local, skip_local, devices, rows)
    arranged = proj.T.reshape(3, devices, local_width, 1, rows)
    streams = lax.all_to_all(arranged, "seq", split_axis=1, concat_axis=3, tiled=True).reshape(
        3, local_width, length
    )
    weight_local = lax.dynamic_slice_in_dim(
        short_weight.reshape(tap_count, 3, channels), first_channel, local_width, 2
    )
    padded = jnp.pad(streams, ((0, 0), (0, 0), (tap_count - 1, 0)))
    filtered = jnp.zeros((3, local_width, length), jnp.float32)
    for tap_index in range(tap_count):
        offset = tap_count - 1 - tap_index
        filtered = filtered + weight_local[tap_index][:, :, None] * padded[
            :, :, offset : offset + length
        ].astype(jnp.float32)
    query_part = filtered[0].reshape(local_width, devices, rows)
    mixed = (filtered[1] * filtered[2]).astype(jnp.bfloat16).reshape(local_width, devices, rows)
    cot_arranged = grad_out.T.reshape(devices, local_width, 1, rows)
    cotangent = lax.all_to_all(
        cot_arranged, "seq", split_axis=0, concat_axis=2, tiled=True
    ).reshape(local_width, devices, rows)
    mixed_spec = forward_transform(mixed, tables)
    conv = inverse_transform(times_kernel(mixed_spec, kernel_re, kernel_im), tables).astype(
        jnp.bfloat16
    )
    gated = (query_part * conv.astype(jnp.float32)).astype(jnp.bfloat16)
    gated_rows = lax.all_to_all(
        gated.reshape(1, local_width, devices, rows), "seq", split_axis=2, concat_axis=0, tiled=True
    )
    gated_output = gated_rows.reshape(channels, rows).T
    scaled = (query_part * cotangent.astype(jnp.float32)).astype(jnp.bfloat16)
    scaled_spec = forward_transform(scaled, tables)
    lag_spec = jnp.stack(
        [
            mixed_spec[0] * scaled_spec[0] + mixed_spec[1] * scaled_spec[1],
            mixed_spec[0] * scaled_spec[1] - mixed_spec[1] * scaled_spec[0],
        ]
    )
    lagged = inverse_transform(lag_spec, tables)
    lagged_rows = lax.all_to_all(
        lagged.reshape(1, local_width, devices, rows),
        "seq",
        split_axis=2,
        concat_axis=0,
        tiled=True,
    )
    filter_grad = lagged_rows.reshape(channels, rows).T
    return (gated_output, filter_grad)


def split_pair(value):
    high = value.astype(jnp.bfloat16)
    low = (value - high.astype(jnp.float32)).astype(jnp.bfloat16)
    return (high, low)


def dot32(left, right):
    return jnp.dot(left, right, preferred_element_type=jnp.float32)


def cosines(turns, whole):
    folded = ((turns + whole // 2) & (whole - 1)) - whole // 2
    angle = (2.0 * math.pi / whole) * (whole // 4 - jnp.abs(folded)).astype(jnp.float32)
    square = angle * angle
    series = jnp.full_like(angle, SINE[-1])
    for factor in SINE[-2::-1]:
        series = series * square + factor
    return angle * series


def table_body(devices, rows, forward, backward, outer_forward, outer_backward, twist):
    fine = FINE_PRODUCT // devices
    log_rows, log_fine = rows.bit_length() - 1, fine.bit_length() - 1
    log_product = FINE_PRODUCT.bit_length() - 1
    length = devices * rows

    def fill(out, height, width, value):
        for start in range(0, height, STRIP):
            line = lax.broadcasted_iota(jnp.int32, (STRIP, width), 0) + start
            lane = lax.broadcasted_iota(jnp.int32, (STRIP, width), 1)
            high, low = split_pair(value(line, lane))
            out[start : start + STRIP, :] = high
            out[height + start : height + start + STRIP, :] = low

    def base(sign):
        def value(line, lane):
            quarter = ((line >> log_rows) - (lane >> log_rows)) * (sign * (rows // 4))
            return cosines((line & (rows - 1)) * (lane & (rows - 1)) + quarter, rows)

        return value

    def outer(line, lane):
        coarse = (line & (FINE_PRODUCT - 1)) >> log_fine
        turns = (2 * coarse + 1) * (lane >> log_fine) + (line >> log_product) * devices
        same = (line & (fine - 1)) == (lane & (fine - 1))
        return jnp.where(same, cosines(turns, 4 * devices), 0.0)

    def outer_back(line, lane):
        coarse = (lane & (FINE_PRODUCT - 1)) >> log_fine
        position = line >> log_fine
        turns = (2 * coarse + 1) * position + (lane >> log_product) * devices
        same = (line & (fine - 1)) == (lane & (fine - 1))
        return jnp.where(same, cosines(turns, 4 * devices) * (1.0 / length), 0.0)

    fill(forward, 2 * rows, 2 * rows, base(1))
    fill(backward, 2 * rows, 2 * rows, base(-1))
    fill(outer_forward, 2 * FINE_PRODUCT, FINE_PRODUCT, outer)
    fill(outer_backward, FINE_PRODUCT, 2 * FINE_PRODUCT, outer_back)
    for start in range(0, FINE_PRODUCT, STRIP):
        line = lax.broadcasted_iota(jnp.int32, (STRIP, LANES), 0) + start
        odd = 2 * (line >> log_fine) + 1
        for index, turns in enumerate((odd * (line & (fine - 1)), odd * fine)):
            twist[2 * index, start : start + STRIP, :] = cosines(turns, 4 * length)
            twist[2 * index + 1, start : start + STRIP, :] = cosines(turns - length, 4 * length)


def spectral_tables(devices, rows, earlier):
    whole = lambda shape: pl.BlockSpec(shape, lambda g: (0,) * len(shape))
    shapes = [
        jax.ShapeDtypeStruct((4 * rows, 2 * rows), jnp.bfloat16),
        jax.ShapeDtypeStruct((4 * rows, 2 * rows), jnp.bfloat16),
        jax.ShapeDtypeStruct((4 * FINE_PRODUCT, FINE_PRODUCT), jnp.bfloat16),
        jax.ShapeDtypeStruct((2 * FINE_PRODUCT, 2 * FINE_PRODUCT), jnp.bfloat16),
        jax.ShapeDtypeStruct((4, FINE_PRODUCT, LANES), jnp.float32),
    ]
    return pl.pallas_call(
        lambda earlier, *outs: table_body(devices, rows, *outs),
        grid=(1,),
        in_specs=[pl.BlockSpec(memory_space=pl.ANY)],
        out_specs=[whole(one.shape) for one in shapes],
        out_shape=shapes,
        cost_estimate=pl.CostEstimate(
            flops=1000, transcendentals=0, bytes_accessed=1000
        ),
        name="tables",
    )(earlier)


def mix_body(
    plain, where, query_in, key_in, value_in, before_q, before_k, before_v,
    weight_q, weight_k, weight_v, cot, *outputs
):
    *sends, query_out, mixed_out, padded = outputs
    taps = weight_q.shape[0]
    rows = query_in.shape[0]
    tail = before_q.shape[0]
    plane, rank = where[0], where[1]
    streams = ((query_in, before_q, weight_q), (key_in, before_k, weight_k), (value_in, before_v, weight_v))
    for index, (block, before, _) in enumerate(streams):
        padded[index, :tail, :] = before[...].astype(jnp.float32)
        padded[index, tail:, :] = block[...].astype(jnp.float32)

    def work(piece, sent, slot):
        if isinstance(piece, int):
            lanes = slice(piece * LANES, (piece + 1) * LANES)
        else:
            lanes = pl.ds(pl.multiple_of(piece * LANES, LANES), LANES)
        filtered = []
        for stream, (_, _, weight) in enumerate(streams):
            total = None
            for tap in range(taps):
                term = weight[tap : tap + 1, lanes] * padded[stream, tail - tap : tail - tap + rows, lanes]
                total = term if total is None else total + term
            filtered.append(total)
        mixed = (filtered[1] * filtered[2]).astype(jnp.bfloat16)
        scaled = (filtered[0] * cot[:, lanes].astype(jnp.float32)).astype(jnp.bfloat16)
        query_out[:, lanes] = filtered[0]
        mixed_out[:, lanes] = mixed
        sent[slot, :, :LANES] = mixed
        sent[slot, :, LANES:] = scaled

    if plain:
        for piece in range(sends[0].shape[0]):
            work(piece, sends[0], piece)
    else:
        for index in range(PAIR):
            for side in range(PLANE):
                work(PLANE * index + (rank ^ side), sends[side], index ^ (plane % PAIR))


def mix_streams(where, proj, before, short_weight, grad_out, chunk, chunks, devices, plain):
    rows, channels = grad_out.shape
    taps = short_weight.shape[0]
    tail = before.shape[0]
    step = PAIR * PLANE * LANES
    steps = channels // chunks // step
    base = chunk * steps
    stride = channels // step

    def stream_spec(height, stream):
        return pl.BlockSpec((height, step), lambda g, w, s=stream: (0, s * stride + base + g))

    if plain:
        send_specs = [pl.BlockSpec((PAIR * PLANE, rows, 2 * LANES), lambda g, w: (g, 0, 0))]
        send_shapes = [jax.ShapeDtypeStruct((devices, rows, 2 * LANES), jnp.bfloat16)]
    else:
        send_specs = [
            pl.BlockSpec((PAIR, rows, 2 * LANES), lambda g, w: (g ^ (w[0] // PAIR), 0, 0))
        ] * PLANE
        send_shapes = [
            jax.ShapeDtypeStruct((devices // PLANE, rows, 2 * LANES), jnp.bfloat16)
        ] * PLANE
    *sends, query, mixed = pl.pallas_call(
        functools.partial(mix_body, plain),
        grid_spec=pltpu.PrefetchScalarGridSpec(
            num_scalar_prefetch=1,
            grid=(steps,),
            in_specs=[stream_spec(rows, s) for s in range(3)]
            + [stream_spec(tail, s) for s in range(3)]
            + [stream_spec(taps, s) for s in range(3)]
            + [pl.BlockSpec((rows, step), lambda g, w: (0, base + g))],
            out_specs=send_specs
            + [
                pl.BlockSpec((rows, step), lambda g, w: (0, g)),
                pl.BlockSpec((rows, step), lambda g, w: (0, g)),
            ],
            scratch_shapes=[pltpu.VMEM((3, tail + rows, step), jnp.float32)],
        ),
        out_shape=send_shapes
        + [
            jax.ShapeDtypeStruct((rows, channels // chunks), jnp.float32),
            jax.ShapeDtypeStruct((rows, channels // chunks), jnp.bfloat16),
        ],
        cost_estimate=pl.CostEstimate(
            flops=3_000_000, transcendentals=0, bytes_accessed=5_000_000
        ),
        name="mix",
    )(where, *[proj] * 3, *[before] * 3, *[short_weight] * 3, grad_out)
    return (sends, query, mixed)


def near_body(mixed, decay, gain, skip, near_out, spread, answer):
    rows, width = mixed.shape
    tiles = width // LANES
    modes = decay.shape[0]
    lines = rows * tiles
    for piece in range(tiles):
        lanes = slice(piece * LANES, (piece + 1) * LANES)
        block = mixed[:, lanes].astype(jnp.float32)
        spread[pl.ds(piece, rows, stride=tiles), :] = block
    for group in range(tiles // 8):
        part = slice(group * 8, group * 8 + 8)
        decays = [decay[r, part, :] for r in range(modes)]
        gains = [gain[r, part, :] for r in range(modes)]
        direct = skip[part, :]

        def step(t, states, group=group, decays=decays, gains=gains, direct=direct):
            at = pl.ds(pl.multiple_of(t * tiles + group * 8, 8), 8)
            here = spread[at, :]
            states = [d * h + here for d, h in zip(decays, states)]
            terms = [g * h for g, h in zip(gains, states)] + [direct * here]
            while len(terms) > 1:
                terms = [a + b for a, b in zip(terms[::2], terms[1::2])] + (
                    terms[-1:] if len(terms) % 2 else []
                )
            answer[at, :] = terms[0]
            return states

        start = [jnp.zeros((8, LANES), jnp.float32)] * modes
        lax.fori_loop(0, rows, step, start, unroll=4)
    for piece in range(tiles):
        lanes = slice(piece * LANES, (piece + 1) * LANES)
        near_out[:, lanes] = answer[pl.ds(piece, rows, stride=tiles), :]


def near_part(mixed, decay, gain, skip, chunk):
    rows, width = mixed.shape
    modes, tiles = decay.shape[0], width // LANES
    return pl.pallas_call(
        near_body,
        grid=(1,),
        in_specs=[
            pl.BlockSpec((rows, width), lambda g: (0, 0)),
            pl.BlockSpec((modes, tiles, LANES), lambda g: (0, chunk, 0)),
            pl.BlockSpec((modes, tiles, LANES), lambda g: (0, chunk, 0)),
            pl.BlockSpec((tiles, LANES), lambda g: (chunk, 0)),
        ],
        out_specs=pl.BlockSpec((rows, width), lambda g: (0, 0)),
        out_shape=jax.ShapeDtypeStruct((rows, width), jnp.float32),
        scratch_shapes=[
            pltpu.VMEM((rows * tiles, LANES), jnp.float32),
            pltpu.VMEM((rows * tiles, LANES), jnp.float32),
        ],
        cost_estimate=pl.CostEstimate(flops=1000, transcendentals=0, bytes_accessed=1000),
        name="near",
    )(mixed, decay, gain, skip)


def lag_body(count, where, *refs):
    sources = refs[:count]
    (rate, amplitude, forward, backward, outer_forward, outer_backward, twist) = refs[count : count + 7]
    (out, stacked, lined, high, low, back, turns, leads) = refs[count + 7 :]
    plane, rank = where[0], where[1]
    devices, rows = lined.shape[0], lined.shape[1]
    fine = FINE_PRODUCT // devices
    groups = rows // fine
    modes = rate.shape[0]

    def place(position, whole):
        at = pl.ds(pl.multiple_of(position * fine, fine), fine)
        for group in range(groups):
            stacked[group, at, :] = whole[group * fine : (group + 1) * fine, :]
        lined[position] = whole[:, :LANES].astype(jnp.float32)

    if count == 1:
        for position in range(devices):
            place(position, sources[0][position])
    else:
        for turned in range(devices // PLANE):
            for side in range(PLANE):
                whole = sources[side][0] if turned == 0 else sources[PLANE - 1 + turned][side]
                place(PLANE * (turned ^ plane) + (side ^ rank), whole)

    def store(line, at, value):
        out[line, at, :] = value

    turns[0, 0] = twist[0]
    turns[0, 1] = twist[1]
    for group in range(1, groups):
        cos, sin = turns[group - 1, 0], turns[group - 1, 1]
        turns[group, 0] = cos * twist[2] - sin * twist[3]
        turns[group, 1] = sin * twist[2] + cos * twist[3]

    def outer_step(group, carry):
        signal = stacked[group]
        first = dot32(outer_forward[: 2 * FINE_PRODUCT, :], signal) + dot32(
            outer_forward[2 * FINE_PRODUCT :, :], signal
        )
        cos, sin = turns[group, 0], turns[group, 1]
        cos = jnp.concatenate([cos, cos], axis=1)
        sin = jnp.concatenate([sin, sin], axis=1)
        real, imag = first[:FINE_PRODUCT], first[FINE_PRODUCT:]
        pairs = (split_pair(real * cos + imag * sin), split_pair(imag * cos - real * sin))
        for k in range(devices):
            source = slice(k * fine, (k + 1) * fine)
            for part in range(2):
                at = pl.ds(pl.multiple_of(part * rows + group * fine, fine), fine)
                high[k, at, :] = pairs[part][0][source, :]
                low[k, at, :] = pairs[part][1][source, :]
        return carry

    lax.fori_loop(0, groups, outer_step, 0, unroll=4)

    def inner_step(k, carry):
        spectrum = (
            dot32(forward[: 2 * rows], high[k])
            + dot32(forward[: 2 * rows], low[k])
            + dot32(forward[2 * rows :], high[k])
        )
        real_m, imag_m = spectrum[:rows, :LANES], spectrum[rows:, :LANES]
        real_s, imag_s = spectrum[:rows, LANES:], spectrum[rows:, LANES:]
        product = jnp.concatenate(
            [real_m * real_s + imag_m * imag_s, real_m * imag_s - imag_m * real_s], axis=0
        )
        prod_high, prod_low = split_pair(product)
        lagged = (
            dot32(backward[: 2 * rows], prod_high)
            + dot32(backward[: 2 * rows], prod_low)
            + dot32(backward[2 * rows :], prod_high)
        )
        for group in range(groups):
            for part in range(2):
                source = slice(part * rows + group * fine, part * rows + (group + 1) * fine)
                at = pl.ds(pl.multiple_of(part * FINE_PRODUCT + k * fine, fine), fine)
                back[group, at, :] = lagged[source, :]
        return carry

    lax.fori_loop(0, devices, inner_step, 0, unroll=UNROLL)

    decay = jnp.exp(-rate[...])

    def advance(t, states):
        result = []
        for p in range(devices):
            here = jnp.broadcast_to(lined[p, pl.ds(t, 1), :], (modes, LANES))
            result.append(decay * states[p] + here)
        return tuple(result)

    start = tuple(jnp.zeros((modes, LANES), jnp.float32) for _ in range(devices))
    ends = lax.fori_loop(0, rows, advance, start, unroll=8)
    far = jnp.exp(-float(rows) * rate[...])
    lead = amplitude[...] * decay
    carried = jnp.zeros((modes, LANES), jnp.float32)
    for p in range(devices):
        send_high, send_low = split_pair(lead * carried)
        leads[p, :modes, :] = send_high
        leads[p, modes:, :] = send_low
        carried = far * carried + ends[p]
    for line in range(devices):
        store(line, slice(rows, rows + 2 * modes), leads[line])

    def last_step(group, carry):
        cos, sin = turns[group, 0], turns[group, 1]
        real, imag = back[group, :FINE_PRODUCT, :], back[group, FINE_PRODUCT:, :]
        turned_back = jnp.concatenate([real * cos - imag * sin, real * sin + imag * cos], axis=0)
        back_high, back_low = split_pair(turned_back)
        result = (
            dot32(outer_backward[:FINE_PRODUCT, :], back_high)
            + dot32(outer_backward[:FINE_PRODUCT, :], back_low)
            + dot32(outer_backward[FINE_PRODUCT:, :], back_high)
        ).astype(jnp.bfloat16)
        at = pl.ds(pl.multiple_of(group * fine, fine), fine)
        for line in range(devices):
            store(line, at, result[line * fine : (line + 1) * fine, :])
        return carry

    lax.fori_loop(0, groups, last_step, 0, unroll=4)


def lag_part(where, sources, rate, amplitude, tables, devices):
    rows = sources[0].shape[-2]
    modes = rate.shape[0]
    groups = rows * devices // FINE_PRODUCT
    height = rows + 2 * modes
    count = len(sources)
    whole = lambda shape: pl.BlockSpec(shape, lambda g, w: (0,) * len(shape))
    if count == 1:
        source_specs = [whole(sources[0].shape)]
    else:
        source_specs = [whole((1, rows, 2 * LANES))] * PLANE
        source_specs += [whole(one.shape) for one in sources[PLANE:]]
    out_shape = jax.ShapeDtypeStruct((devices, height, LANES), jnp.bfloat16)
    return pl.pallas_call(
        functools.partial(lag_body, count),
        grid_spec=pltpu.PrefetchScalarGridSpec(
            num_scalar_prefetch=1,
            grid=(1,),
            in_specs=source_specs
            + [whole((modes, LANES))] * 2
            + [whole(table.shape) for table in tables],
            out_specs=whole(out_shape.shape),
            scratch_shapes=[
                pltpu.VMEM((groups, FINE_PRODUCT, 2 * LANES), jnp.bfloat16),
                pltpu.VMEM((devices, rows, LANES), jnp.float32),
                pltpu.VMEM((devices, 2 * rows, 2 * LANES), jnp.bfloat16),
                pltpu.VMEM((devices, 2 * rows, 2 * LANES), jnp.bfloat16),
                pltpu.VMEM((groups, 2 * FINE_PRODUCT, LANES), jnp.float32),
                pltpu.VMEM((groups, 2, FINE_PRODUCT, LANES), jnp.float32),
                pltpu.VMEM((devices, 2 * modes, LANES), jnp.bfloat16),
            ],
        ),
        out_shape=out_shape,
        cost_estimate=pl.CostEstimate(
            flops=60_000_000_000, transcendentals=0, bytes_accessed=12_000_000
        ),
        name="lags",
    )(where, *sources, rate, amplitude, *tables)


def finish_body(arrived, near, query, decay, *refs):
    gated_out, grad_out = refs[-2:]
    rows = near.shape[0]
    modes = decay.shape[0]
    line = lax.broadcasted_iota(jnp.int32, (8, LANES), 0)

    def work(column):
        at = slice(column * LANES, (column + 1) * LANES)
        block = arrived.at[column]
        grad_out[:, at] = block[:rows, :].astype(jnp.float32)
        lead = block[rows : rows + modes, :].astype(jnp.float32) + block[
            rows + modes : rows + 2 * modes, :
        ].astype(jnp.float32)
        total = [near[8 * tile : 8 * tile + 8, at] for tile in range(rows // 8)]
        rate_here = decay[:, at]
        for mode in range(modes):
            d1 = jnp.broadcast_to(rate_here[mode : mode + 1, :], (8, LANES))
            d2 = d1 * d1
            d4 = d2 * d2
            d8 = d4 * d4
            ones = jnp.ones_like(d1)
            power = (
                jnp.where(line & 1 != 0, d1, ones)
                * jnp.where(line & 2 != 0, d2, ones)
                * jnp.where(line & 4 != 0, d4, ones)
            )
            term = power * lead[mode : mode + 1, :]
            for tile in range(rows // 8):
                total[tile] = total[tile] + term
                if tile + 1 < rows // 8:
                    term = term * d8
        conv = jnp.concatenate(total, axis=0).astype(jnp.bfloat16)
        gated_out[:, at] = (query[:, at] * conv.astype(jnp.float32)).astype(jnp.bfloat16)

    for column in range(PAIR * PLANE):
        work(column)


def finish_part(arrived, near, query, decay, previous, chunk, chunks):
    rows, width = near.shape
    modes = decay.shape[0]
    step = PAIR * PLANE * LANES
    steps = width // step
    here = lambda g: (0, chunk * steps + g)
    in_specs = [
        pl.BlockSpec((PAIR * PLANE, arrived.shape[1], LANES), lambda g: (g, 0, 0)),
        pl.BlockSpec((rows, step), lambda g: (0, g)),
        pl.BlockSpec((rows, step), lambda g: (0, g)),
        pl.BlockSpec((modes, step), here),
    ]
    args = [arrived, near, query, decay]
    aliases = {}
    if previous is not None:
        in_specs += [pl.BlockSpec(memory_space=pl.ANY)] * 2
        aliases = {len(args): 0, len(args) + 1: 1}
        args += list(previous)
    return pl.pallas_call(
        finish_body,
        grid=(steps,),
        in_specs=in_specs,
        out_specs=[pl.BlockSpec((rows, step), here)] * 2,
        out_shape=[
            jax.ShapeDtypeStruct((rows, width * chunks), jnp.bfloat16),
            jax.ShapeDtypeStruct((rows, width * chunks), jnp.float32),
        ],
        input_output_aliases=aliases,
        cost_estimate=pl.CostEstimate(flops=1000, transcendentals=0, bytes_accessed=1000),
        name="finish",
    )(*args)


def swap(value, mask, devices):
    return lax.ppermute(value, "seq", [(i, i ^ mask) for i in range(devices)])


def after(value, *earlier):
    return lax.optimization_barrier((value, earlier))[0]


def share(parts, devices):
    return [parts[0]] + [swap(parts[side], side, devices) for side in range(1, PLANE)]


def spread_out(shared, devices):
    return [
        swap(jnp.concatenate([one[k : k + 1] for one in shared], axis=0), PLANE * k, devices)
        for k in range(1, devices // PLANE)
    ]


def all_to_all(sent):
    return lax.all_to_all(sent, "seq", split_axis=0, concat_axis=0, tiled=True)


def fast_on_device(proj, short_weight, residues, rates, skip, grad_out):
    devices = lax.axis_size("seq")
    rows, channels = grad_out.shape
    modes = rates.shape[0]
    width = channels // 2
    me = lax.axis_index("seq")
    where = jnp.stack([me // PLANE, me % PLANE]).astype(jnp.int32)
    before = lax.ppermute(
        proj[rows - HALO :], "seq", [(i, i + 1) for i in range(devices - 1)]
    )
    streams = (proj, before, short_weight, grad_out)
    (sent,), query_a, mixed_a = mix_streams(where, *streams, 0, 2, devices, True)
    arrived = all_to_all(sent)
    parts, query_b, mixed_b = mix_streams(after(where, sent), *streams, 1, 2, devices, False)
    shared = share(parts, devices)
    tables = spectral_tables(devices, rows, parts[0])
    rates, residues, skip = after((rates, residues, skip), parts)
    decay = jnp.exp(-rates)
    amplitude = residues * jnp.sqrt(rates)
    tiles = (modes, channels // LANES, LANES)
    params = (decay.reshape(tiles), amplitude.reshape(tiles), skip.reshape(tiles[1:]))
    near_a = near_part(mixed_a, *params, 0)
    shared = after(shared, near_a, tables)
    moved = spread_out(shared, devices)

    def lags(guard, sources, chunk):
        start = chunk * width + me * LANES
        rate = lax.dynamic_slice_in_dim(rates, start, LANES, 1)
        lead = lax.dynamic_slice_in_dim(amplitude, start, LANES, 1)
        return lag_part(after(where, guard), sources, rate, lead, tables, devices)

    back_a = lags(shared[0], [arrived], 0)
    arrived_a = all_to_all(back_a)
    back_b = lags(back_a, [*shared, *moved], 1)
    arrived_b = all_to_all(back_b)
    near_b = near_part(after(mixed_b, back_b), *params, 1)
    result = finish_part(arrived_a, near_a, query_a, decay, None, 0, 2)
    result = finish_part(arrived_b, near_b, query_b, decay, result, 1, 2)
    return tuple(result)


def solution(mesh):
    def body(proj, short_weight, residues, rates, skip, grad_out):
        devices = lax.axis_size("seq")
        rows, channels = grad_out.shape
        fits = (
            devices in (8, 16)
            and rows % LANES == 0
            and channels == 2 * devices * LANES
            and residues.shape[0] == 16
            and short_weight.shape[0] <= HALO + 1
        )
        chosen = fast_on_device if fits else on_device
        return chosen(proj, short_weight, residues, rates, skip, grad_out)

    return jax.shard_map(
        body,
        mesh=mesh,
        in_specs=(P(("groups", "seq"), None), P(), P(), P(), P(), P(("groups", "seq"), None)),
        out_specs=(P(("groups", "seq"), None), P(("groups", "seq"), None)),
        check_vma=False,
    )
```

```python
import functools
import math

import jax
import jax.numpy as jnp
from jax import lax
from jax.experimental import pallas as pl
from jax.experimental.pallas import tpu as pltpu
from jax.sharding import PartitionSpec as P

HIGH_PRECISION = lax.Precision.HIGH
LANES = 128
HALO = 8
UNROLL = 16
STRIP = 32
PLANE = 4
PAIR = 2
SINE = (1.0, -1.0 / 6, 1.0 / 120, -1.0 / 5040, 1.0 / 362880, -1.0 / 39916800, 1.0 / 6227020800)


def make_tables(devices, rows):
    length = devices * rows
    halves = jnp.arange(2, dtype=jnp.int32)
    coarse = jnp.arange(devices, dtype=jnp.int32)
    fine_pos = jnp.arange(rows, dtype=jnp.int32)
    outer_turn = (
        coarse[None, None, :] * (2 * coarse[None, :, None] + halves[:, None, None]) % (2 * devices)
    )
    outer_angle = -math.pi / devices * outer_turn.astype(jnp.float32)
    twist_turn = (
        fine_pos[None, None, :] * (2 * coarse[None, :, None] + halves[:, None, None]) % (2 * length)
    )
    twist_angle = -math.pi / length * twist_turn.astype(jnp.float32)
    inner_turn = fine_pos[:, None] * fine_pos[None, :] % rows
    inner_angle = -2.0 * math.pi / rows * inner_turn.astype(jnp.float32)
    outer_stack = jnp.stack([jnp.cos(outer_angle), jnp.sin(outer_angle)])
    inverse_outer = outer_stack * (0.5 / length)
    inner_cos = jnp.cos(inner_angle)
    inner_sin = jnp.sin(inner_angle)
    forward_inner = jnp.stack(
        [jnp.stack([inner_cos, -inner_sin]), jnp.stack([inner_sin, inner_cos])]
    )
    inverse_inner = jnp.stack(
        [jnp.stack([inner_cos, inner_sin]), jnp.stack([-inner_sin, inner_cos])]
    )
    return (
        outer_stack,
        inverse_outer,
        jnp.cos(twist_angle)[:, None],
        jnp.sin(twist_angle)[:, None],
        forward_inner,
        inverse_inner,
    )


def forward_transform(signal, tables):
    outer_stack, inverse_outer, twist_re, twist_im, forward_inner, inverse_inner = tables
    first = jnp.einsum(
        "rbkp,cpj->rbckj", outer_stack, signal.astype(jnp.float32), precision=HIGH_PRECISION
    )
    turned = jnp.stack(
        [first[0] * twist_re - first[1] * twist_im, first[0] * twist_im + first[1] * twist_re]
    )
    return jnp.einsum("rsmj,sbckj->rbckm", forward_inner, turned, precision=HIGH_PRECISION)


def inverse_transform(spectrum, tables):
    outer_stack, inverse_outer, twist_re, twist_im, forward_inner, inverse_inner = tables
    back = jnp.einsum("rsjm,sbckm->rbckj", inverse_inner, spectrum, precision=HIGH_PRECISION)
    turned = jnp.stack(
        [back[0] * twist_re + back[1] * twist_im, back[1] * twist_re - back[0] * twist_im]
    )
    return jnp.einsum("rbkp,rbckj->cpj", inverse_outer, turned, precision=HIGH_PRECISION)


def filter_spectrum(residue_local, rate_local, skip_local, devices, rows):
    length = devices * rows
    halves = jnp.arange(2, dtype=jnp.int32)[:, None, None, None]
    coarse = jnp.arange(devices, dtype=jnp.int32)[None, None, :, None]
    fine_pos = jnp.arange(rows, dtype=jnp.int32)[None, None, None, :]
    frequency = 2 * (coarse + devices * fine_pos) + halves
    half_angle = math.pi / (2 * length) * frequency.astype(jnp.float32)
    sine_half = jnp.sin(half_angle)
    sine_sq = sine_half * sine_half
    sine_full = 2.0 * sine_half * jnp.cos(half_angle)
    parity_sign = (1 - 2 * halves).astype(jnp.float32)
    local_width = residue_local.shape[1]
    kernel_re = jnp.zeros((2, local_width, devices, rows), jnp.float32)
    kernel_im = jnp.zeros((2, local_width, devices, rows), jnp.float32)
    for mode_index in range(residue_local.shape[0]):
        rate_row = rate_local[mode_index][None, :, None, None]
        amplitude = residue_local[mode_index][None, :, None, None] * jnp.sqrt(rate_row)
        decay_factor = jnp.exp(-rate_row)
        decay_gap = -jnp.expm1(-rate_row)
        tail_factor = jnp.exp(-rate_row * length)
        denominator = decay_gap * decay_gap + 4.0 * decay_factor * sine_sq
        weighting = amplitude * (1.0 - tail_factor * parity_sign) / denominator
        kernel_re = kernel_re + weighting * (decay_gap + 2.0 * decay_factor * sine_sq)
        kernel_im = kernel_im - weighting * decay_factor * sine_full
    kernel_re = kernel_re + skip_local[None, :, None, None]
    return (kernel_re, kernel_im)


def times_kernel(spectrum, kernel_re, kernel_im):
    return jnp.stack(
        [
            spectrum[0] * kernel_re - spectrum[1] * kernel_im,
            spectrum[0] * kernel_im + spectrum[1] * kernel_re,
        ]
    )


def on_device(proj, short_weight, residues, rates, skip, grad_out):
    devices = lax.axis_size("seq")
    rows = proj.shape[0]
    channels = grad_out.shape[1]
    local_width = channels // devices
    length = devices * rows
    tap_count = short_weight.shape[0]
    first_channel = lax.axis_index("seq") * local_width
    residue_local = lax.dynamic_slice_in_dim(residues, first_channel, local_width, 1)
    rate_local = lax.dynamic_slice_in_dim(rates, first_channel, local_width, 1)
    skip_local = lax.dynamic_slice_in_dim(skip, first_channel, local_width, 0)
    tables = make_tables(devices, rows)
    kernel_re, kernel_im = filter_spectrum(residue_local, rate_local, skip_local, devices, rows)
    arranged = proj.T.reshape(3, devices, local_width, 1, rows)
    streams = lax.all_to_all(arranged, "seq", split_axis=1, concat_axis=3, tiled=True).reshape(
        3, local_width, length
    )
    weight_local = lax.dynamic_slice_in_dim(
        short_weight.reshape(tap_count, 3, channels), first_channel, local_width, 2
    )
    padded = jnp.pad(streams, ((0, 0), (0, 0), (tap_count - 1, 0)))
    filtered = jnp.zeros((3, local_width, length), jnp.float32)
    for tap_index in range(tap_count):
        offset = tap_count - 1 - tap_index
        filtered = filtered + weight_local[tap_index][:, :, None] * padded[
            :, :, offset : offset + length
        ].astype(jnp.float32)
    query_part = filtered[0].reshape(local_width, devices, rows)
    mixed = (filtered[1] * filtered[2]).astype(jnp.bfloat16).reshape(local_width, devices, rows)
    cot_arranged = grad_out.T.reshape(devices, local_width, 1, rows)
    cotangent = lax.all_to_all(
        cot_arranged, "seq", split_axis=0, concat_axis=2, tiled=True
    ).reshape(local_width, devices, rows)
    mixed_spec = forward_transform(mixed, tables)
    conv = inverse_transform(times_kernel(mixed_spec, kernel_re, kernel_im), tables).astype(
        jnp.bfloat16
    )
    gated = (query_part * conv.astype(jnp.float32)).astype(jnp.bfloat16)
    gated_rows = lax.all_to_all(
        gated.reshape(1, local_width, devices, rows), "seq", split_axis=2, concat_axis=0, tiled=True
    )
    gated_output = gated_rows.reshape(channels, rows).T
    scaled = (query_part * cotangent.astype(jnp.float32)).astype(jnp.bfloat16)
    scaled_spec = forward_transform(scaled, tables)
    lag_spec = jnp.stack(
        [
            mixed_spec[0] * scaled_spec[0] + mixed_spec[1] * scaled_spec[1],
            mixed_spec[0] * scaled_spec[1] - mixed_spec[1] * scaled_spec[0],
        ]
    )
    lagged = inverse_transform(lag_spec, tables)
    lagged_rows = lax.all_to_all(
        lagged.reshape(1, local_width, devices, rows),
        "seq",
        split_axis=2,
        concat_axis=0,
        tiled=True,
    )
    filter_grad = lagged_rows.reshape(channels, rows).T
    return (gated_output, filter_grad)


def split_pair(value):
    high = value.astype(jnp.bfloat16)
    low = (value - high.astype(jnp.float32)).astype(jnp.bfloat16)
    return (high, low)


def dot32(left, right):
    return jnp.dot(left, right, preferred_element_type=jnp.float32)


def cosines(turns, whole):
    folded = ((turns + whole // 2) & (whole - 1)) - whole // 2
    angle = (2.0 * math.pi / whole) * (whole // 4 - jnp.abs(folded)).astype(jnp.float32)
    square = angle * angle
    series = jnp.full_like(angle, SINE[-1])
    for factor in SINE[-2::-1]:
        series = series * square + factor
    return angle * series


def table_body(devices, rows, forward, backward, twist):
    log_rows = rows.bit_length() - 1
    length = devices * rows

    def fill(out, height, width, value):
        for start in range(0, height, STRIP):
            line = lax.broadcasted_iota(jnp.int32, (STRIP, width), 0) + start
            lane = lax.broadcasted_iota(jnp.int32, (STRIP, width), 1)
            high, low = split_pair(value(line, lane))
            out[start : start + STRIP, :] = high
            out[height + start : height + start + STRIP, :] = low

    def base(sign):
        def value(line, lane):
            quarter = ((line >> log_rows) - (lane >> log_rows)) * (sign * (rows // 4))
            return cosines((line & (rows - 1)) * (lane & (rows - 1)) + quarter, rows)

        return value

    fill(forward, 2 * rows, 2 * rows, base(1))
    fill(backward, 2 * rows, 2 * rows, base(-1))
    line = lax.broadcasted_iota(jnp.int32, (8 * devices, LANES), 0)
    turns = (4 * (line >> 3) + 1) * (line & 7)
    twist[0] = cosines(turns, 4 * length)
    twist[1] = cosines(turns - length, 4 * length)


def spectral_tables(devices, rows, earlier):
    whole = lambda shape: pl.BlockSpec(shape, lambda g: (0,) * len(shape))
    shapes = [
        jax.ShapeDtypeStruct((4 * rows, 2 * rows), jnp.bfloat16),
        jax.ShapeDtypeStruct((4 * rows, 2 * rows), jnp.bfloat16),
        jax.ShapeDtypeStruct((2, 8 * devices, LANES), jnp.float32),
    ]
    return pl.pallas_call(
        lambda earlier, *outs: table_body(devices, rows, *outs),
        grid=(1,),
        in_specs=[pl.BlockSpec(memory_space=pl.ANY)],
        out_specs=[whole(one.shape) for one in shapes],
        out_shape=shapes,
        cost_estimate=pl.CostEstimate(
            flops=1000, transcendentals=0, bytes_accessed=1000
        ),
        name="tables",
    )(earlier)


def mix_body(
    plain, skipped, where, query_in, key_in, value_in, before_q, before_k, before_v,
    weight_q, weight_k, weight_v, cot, *outputs
):
    *sends, query_out, mixed_out, padded = outputs[skipped:]
    taps = weight_q.shape[0]
    rows = query_in.shape[0]
    tail = before_q.shape[0]
    plane, rank = where[0], where[1]
    streams = ((query_in, before_q, weight_q), (key_in, before_k, weight_k), (value_in, before_v, weight_v))
    for index, (block, before, _) in enumerate(streams):
        padded[index, :tail, :] = before[...].astype(jnp.float32)
        padded[index, tail:, :] = block[...].astype(jnp.float32)

    def work(piece, sent, slot):
        if isinstance(piece, int):
            lanes = slice(piece * LANES, (piece + 1) * LANES)
        else:
            lanes = pl.ds(pl.multiple_of(piece * LANES, LANES), LANES)
        filtered = []
        for stream, (_, _, weight) in enumerate(streams):
            total = None
            for tap in range(taps):
                term = weight[tap : tap + 1, lanes] * padded[stream, tail - tap : tail - tap + rows, lanes]
                total = term if total is None else total + term
            filtered.append(total)
        mixed = (filtered[1] * filtered[2]).astype(jnp.bfloat16)
        scaled = (filtered[0] * cot[:, lanes].astype(jnp.float32)).astype(jnp.bfloat16)
        query_out[:, lanes] = filtered[0]
        mixed_out[:, lanes] = mixed
        sent[slot, :, :LANES] = mixed
        sent[slot, :, LANES:] = scaled

    if plain:
        for piece in range(sends[0].shape[0]):
            work(piece, sends[0], piece)
    else:
        for index in range(PAIR):
            for side in range(PLANE):
                work(PLANE * index + (rank ^ side), sends[side], index ^ (plane % PAIR))


def mix_streams(
    where, proj, before, short_weight, grad_out, chunk, chunks, devices, plain, top=None, earlier=None
):
    full, channels = grad_out.shape
    rows = full if top is None else top
    taps = short_weight.shape[0]
    tail = HALO
    step = PAIR * PLANE * LANES
    steps = channels // chunks // step
    base = chunk * steps
    stride = channels // step

    def stream_spec(height, stream):
        return pl.BlockSpec((height, step), lambda g, w, s=stream: (0, s * stride + base + g))

    if plain:
        send_specs = [pl.BlockSpec((PAIR * PLANE, rows, 2 * LANES), lambda g, w: (g, 0, 0))]
        send_shapes = [jax.ShapeDtypeStruct((devices, full, 2 * LANES), jnp.bfloat16)]
    else:
        send_specs = [
            pl.BlockSpec((PAIR, rows, 2 * LANES), lambda g, w: (g ^ (w[0] // PAIR), 0, 0))
        ] * PLANE
        send_shapes = [
            jax.ShapeDtypeStruct((devices // PLANE, full, 2 * LANES), jnp.bfloat16)
        ] * PLANE
    earlier = () if earlier is None else earlier
    operands = (*[proj] * 3, *[before] * 3, *[short_weight] * 3, grad_out)
    *sends, query, mixed = pl.pallas_call(
        functools.partial(mix_body, plain, len(earlier)),
        grid_spec=pltpu.PrefetchScalarGridSpec(
            num_scalar_prefetch=1,
            grid=(steps,),
            in_specs=[stream_spec(rows, s) for s in range(3)]
            + [stream_spec(tail, s) for s in range(3)]
            + [stream_spec(taps, s) for s in range(3)]
            + [pl.BlockSpec((rows, step), lambda g, w: (0, base + g))]
            + [pl.BlockSpec(memory_space=pl.ANY)] * len(earlier),
            out_specs=send_specs
            + [
                pl.BlockSpec((rows, step), lambda g, w: (0, g)),
                pl.BlockSpec((rows, step), lambda g, w: (0, g)),
            ],
            scratch_shapes=[pltpu.VMEM((3, tail + rows, step), jnp.float32)],
        ),
        out_shape=send_shapes
        + [
            jax.ShapeDtypeStruct((full, channels // chunks), jnp.float32),
            jax.ShapeDtypeStruct((full, channels // chunks), jnp.bfloat16),
        ],
        input_output_aliases={len(operands) + 1 + i: i for i in range(len(earlier))},
        cost_estimate=pl.CostEstimate(
            flops=3_000_000, transcendentals=0, bytes_accessed=5_000_000
        ),
        name="mix",
    )(where, *operands, *earlier)
    return (sends, query, mixed)


def near_body(mixed, decay, gain, skip, near_out, spread, answer):
    rows, width = mixed.shape
    tiles = width // LANES
    modes = decay.shape[0]
    lines = rows * tiles
    for piece in range(tiles):
        lanes = slice(piece * LANES, (piece + 1) * LANES)
        block = mixed[:, lanes].astype(jnp.float32)
        spread[pl.ds(piece, rows, stride=tiles), :] = block
    for group in range(tiles // 8):
        part = slice(group * 8, group * 8 + 8)
        decays = [decay[r, part, :] for r in range(modes)]
        gains = [gain[r, part, :] for r in range(modes)]
        direct = skip[part, :]

        def step(t, states, group=group, decays=decays, gains=gains, direct=direct):
            at = pl.ds(pl.multiple_of(t * tiles + group * 8, 8), 8)
            here = spread[at, :]
            states = [d * h + here for d, h in zip(decays, states)]
            terms = [g * h for g, h in zip(gains, states)] + [direct * here]
            while len(terms) > 1:
                terms = [a + b for a, b in zip(terms[::2], terms[1::2])] + (
                    terms[-1:] if len(terms) % 2 else []
                )
            answer[at, :] = terms[0]
            return states

        start = [jnp.zeros((8, LANES), jnp.float32)] * modes
        lax.fori_loop(0, rows, step, start, unroll=4)
    for piece in range(tiles):
        lanes = slice(piece * LANES, (piece + 1) * LANES)
        near_out[:, lanes] = answer[pl.ds(piece, rows, stride=tiles), :]


def near_part(mixed, decay, gain, skip, chunk):
    rows, width = mixed.shape
    modes, tiles = decay.shape[0], width // LANES
    return pl.pallas_call(
        near_body,
        grid=(1,),
        in_specs=[
            pl.BlockSpec((rows, width), lambda g: (0, 0)),
            pl.BlockSpec((modes, tiles, LANES), lambda g: (0, chunk, 0)),
            pl.BlockSpec((modes, tiles, LANES), lambda g: (0, chunk, 0)),
            pl.BlockSpec((tiles, LANES), lambda g: (chunk, 0)),
        ],
        out_specs=pl.BlockSpec((rows, width), lambda g: (0, 0)),
        out_shape=jax.ShapeDtypeStruct((rows, width), jnp.float32),
        scratch_shapes=[
            pltpu.VMEM((rows * tiles, LANES), jnp.float32),
            pltpu.VMEM((rows * tiles, LANES), jnp.float32),
        ],
        cost_estimate=pl.CostEstimate(flops=1000, transcendentals=0, bytes_accessed=1000),
        name="near",
    )(mixed, decay, gain, skip)


def fourier(values, sign):
    size = len(values)
    if size == 1:
        return values
    evens, odds = fourier(values[::2], sign), fourier(values[1::2], sign)
    result = [None] * size
    for k in range(size // 2):
        real, imag = odds[k]
        if 4 * k == size:
            real, imag, sums = imag, real, (-sign, sign)
        else:
            sums = (1, 1)
            cos, sin = math.cos(2 * math.pi * k / size), sign * math.sin(2 * math.pi * k / size)
            if 8 * k in (size, 3 * size):
                root = math.sqrt(0.5)
                up, down = (real + imag) * root, (imag - real) * root
                turned = {(1, 1): (-down, up), (1, -1): (up, down), (-1, 1): (-up, -down), (-1, -1): (down, -up)}
                real, imag = turned[(1 if cos > 0 else -1, 1 if sin > 0 else -1)]
            elif k:
                real, imag = real * cos - imag * sin, real * sin + imag * cos
        even_real, even_imag = evens[k]
        plus = lambda left, right, way: left + right if way > 0 else left - right
        result[k] = (plus(even_real, real, sums[0]), plus(even_imag, imag, sums[1]))
        result[k + size // 2] = (plus(even_real, real, -sums[0]), plus(even_imag, imag, -sums[1]))
    return result


def lag_body(count, where, *refs):
    sources = refs[:count]
    (rate, amplitude, forward, backward, twist) = refs[count : count + 5]
    (out, lined, data, back, plain, spin) = refs[count + 5 :]
    plane, rank = where[0], where[1]
    devices, rows = lined.shape[1], lined.shape[2]
    tiles = rows // 8
    modes = rate.shape[0]
    length = devices * rows

    def place(position, whole):
        for half in range(2):
            lined[half, position] = whole[:, half * LANES : (half + 1) * LANES].astype(jnp.float32)

    if count == 1:
        for position in range(devices):
            place(position, sources[0][position])
    else:
        for turned in range(devices // PLANE):
            for side in range(PLANE):
                if turned == 0:
                    whole = sources[side][0]
                else:
                    pair = (devices // PLANE - 1) * (side // 2) + turned - 1
                    whole = sources[PLANE + pair][side % 2]
                place(PLANE * (turned ^ plane) + (side ^ rank), whole)

    def advance_spin():
        for k in range(devices):
            line = slice(8 * k, 8 * k + 8)
            angle = 2.0 * math.pi * 8 * (4 * k + 1) / (4 * length)
            cos, sin = spin[0, line, :], spin[1, line, :]
            spin[0, line, :] = cos * math.cos(angle) - sin * math.sin(angle)
            spin[1, line, :] = sin * math.cos(angle) + cos * math.sin(angle)

    def outer_step(tile, carry):
        at = pl.ds(pl.multiple_of(tile * 8, 8), 8)
        imag_at = pl.ds(pl.multiple_of(rows + tile * 8, 8), 8)
        for half in range(2):
            lanes = slice(half * LANES, (half + 1) * LANES)
            values = []
            for p in range(devices):
                angle = math.pi * p / (2 * devices)
                here = lined[half, p, at, :]
                values.append((here * math.cos(angle), here * -math.sin(angle)))
            for k, (real, imag) in enumerate(fourier(values, -1)):
                cos, sin = spin[0, 8 * k : 8 * k + 8, :], spin[1, 8 * k : 8 * k + 8, :]
                data[k, at, lanes] = real * cos + imag * sin
                data[k, imag_at, lanes] = imag * cos - real * sin
        advance_spin()
        return carry

    spin[...] = twist[...]
    lax.fori_loop(0, tiles, outer_step, 0)

    def inner_step(k, carry):
        high, low = split_pair(data[k])
        spectrum = (
            dot32(forward[: 2 * rows], high)
            + dot32(forward[: 2 * rows], low)
            + dot32(forward[2 * rows :], high)
        )
        real_m, imag_m = spectrum[:rows, :LANES], spectrum[rows:, :LANES]
        real_s, imag_s = spectrum[:rows, LANES:], spectrum[rows:, LANES:]
        product = jnp.concatenate(
            [real_m * real_s + imag_m * imag_s, real_m * imag_s - imag_m * real_s], axis=0
        )
        prod_high, prod_low = split_pair(product)
        back[k] = (
            dot32(backward[: 2 * rows], prod_high)
            + dot32(backward[: 2 * rows], prod_low)
            + dot32(backward[2 * rows :], prod_high)
        )
        return carry

    lax.fori_loop(0, devices, inner_step, 0, unroll=UNROLL)

    decay = jnp.exp(-rate[...])

    def advance(t, states):
        result = []
        for p in range(devices):
            here = jnp.broadcast_to(lined[0, p, pl.ds(t, 1), :], (modes, LANES))
            result.append(decay * states[p] + here)
        return tuple(result)

    start = tuple(jnp.zeros((modes, LANES), jnp.float32) for _ in range(devices))
    ends = lax.fori_loop(0, rows, advance, start, unroll=8)
    far = jnp.exp(-float(rows) * rate[...])
    lead = amplitude[...] * decay
    carried = jnp.zeros((modes, LANES), jnp.float32)
    for p in range(devices):
        send_high, send_low = split_pair(lead * carried)
        out[p, rows : rows + modes, :] = send_high
        out[p, rows + modes : rows + 2 * modes, :] = send_low
        carried = far * carried + ends[p]

    def last_step(tile, carry):
        at = pl.ds(pl.multiple_of(tile * 8, 8), 8)
        imag_at = pl.ds(pl.multiple_of(rows + tile * 8, 8), 8)
        values = []
        for k in range(devices):
            real, imag = back[k, at, :], back[k, imag_at, :]
            cos, sin = spin[0, 8 * k : 8 * k + 8, :], spin[1, 8 * k : 8 * k + 8, :]
            values.append((real * cos - imag * sin, real * sin + imag * cos))
        for p, (real, imag) in enumerate(fourier(values, 1)):
            angle = math.pi * p / (2 * devices)
            plain[p, at, :] = real * (math.cos(angle) / length) - imag * (math.sin(angle) / length)
        advance_spin()
        return carry

    spin[...] = twist[...]
    lax.fori_loop(0, tiles, last_step, 0)
    for p in range(devices):
        out[p, :rows, :] = plain[p].astype(jnp.bfloat16)


def lag_part(where, sources, rate, amplitude, tables, devices):
    rows = sources[0].shape[-2]
    modes = rate.shape[0]
    height = rows + 2 * modes
    count = len(sources)
    whole = lambda shape: pl.BlockSpec(shape, lambda g, w: (0,) * len(shape))
    if count == 1:
        source_specs = [whole(sources[0].shape)]
    else:
        source_specs = [whole((1, rows, 2 * LANES))] * PLANE
        source_specs += [whole(one.shape) for one in sources[PLANE:]]
    out_shape = jax.ShapeDtypeStruct((devices, height, LANES), jnp.bfloat16)
    return pl.pallas_call(
        functools.partial(lag_body, count),
        grid_spec=pltpu.PrefetchScalarGridSpec(
            num_scalar_prefetch=1,
            grid=(1,),
            in_specs=source_specs
            + [whole((modes, LANES))] * 2
            + [whole(table.shape) for table in tables],
            out_specs=whole(out_shape.shape),
            scratch_shapes=[
                pltpu.VMEM((2, devices, rows, LANES), jnp.float32),
                pltpu.VMEM((devices, 2 * rows, 2 * LANES), jnp.float32),
                pltpu.VMEM((devices, 2 * rows, LANES), jnp.float32),
                pltpu.VMEM((devices, rows, LANES), jnp.float32),
                pltpu.VMEM((2, 8 * devices, LANES), jnp.float32),
            ],
        ),
        out_shape=out_shape,
        cost_estimate=pl.CostEstimate(
            flops=60_000_000_000, transcendentals=0, bytes_accessed=12_000_000
        ),
        name="lags",
    )(where, *sources, rate, amplitude, *tables)


def finish_body(arrived, near, query, decay, *refs):
    gated_out, grad_out = refs[-2:]
    rows = near.shape[0]
    modes = decay.shape[0]
    line = lax.broadcasted_iota(jnp.int32, (8, LANES), 0)

    def work(column):
        at = slice(column * LANES, (column + 1) * LANES)
        block = arrived.at[column]
        grad_out[:, at] = block[:rows, :].astype(jnp.float32)
        lead = block[rows : rows + modes, :].astype(jnp.float32) + block[
            rows + modes : rows + 2 * modes, :
        ].astype(jnp.float32)
        total = [near[8 * tile : 8 * tile + 8, at] for tile in range(rows // 8)]
        rate_here = decay[:, at]
        for mode in range(modes):
            d1 = jnp.broadcast_to(rate_here[mode : mode + 1, :], (8, LANES))
            d2 = d1 * d1
            d4 = d2 * d2
            d8 = d4 * d4
            ones = jnp.ones_like(d1)
            power = (
                jnp.where(line & 1 != 0, d1, ones)
                * jnp.where(line & 2 != 0, d2, ones)
                * jnp.where(line & 4 != 0, d4, ones)
            )
            term = power * lead[mode : mode + 1, :]
            for tile in range(rows // 8):
                total[tile] = total[tile] + term
                if tile + 1 < rows // 8:
                    term = term * d8
        conv = jnp.concatenate(total, axis=0).astype(jnp.bfloat16)
        gated_out[:, at] = (query[:, at] * conv.astype(jnp.float32)).astype(jnp.bfloat16)

    for column in range(PAIR * PLANE):
        work(column)


def finish_part(arrived, near, query, decay, previous, chunk, chunks):
    rows, width = near.shape
    modes = decay.shape[0]
    step = PAIR * PLANE * LANES
    steps = width // step
    here = lambda g: (0, chunk * steps + g)
    in_specs = [
        pl.BlockSpec((PAIR * PLANE, arrived.shape[1], LANES), lambda g: (g, 0, 0)),
        pl.BlockSpec((rows, step), lambda g: (0, g)),
        pl.BlockSpec((rows, step), lambda g: (0, g)),
        pl.BlockSpec((modes, step), here),
    ]
    args = [arrived, near, query, decay]
    aliases = {}
    if previous is not None:
        in_specs += [pl.BlockSpec(memory_space=pl.ANY)] * 2
        aliases = {len(args): 0, len(args) + 1: 1}
        args += list(previous)
    return pl.pallas_call(
        finish_body,
        grid=(steps,),
        in_specs=in_specs,
        out_specs=[pl.BlockSpec((rows, step), here)] * 2,
        out_shape=[
            jax.ShapeDtypeStruct((rows, width * chunks), jnp.bfloat16),
            jax.ShapeDtypeStruct((rows, width * chunks), jnp.float32),
        ],
        input_output_aliases=aliases,
        cost_estimate=pl.CostEstimate(flops=1000, transcendentals=0, bytes_accessed=1000),
        name="finish",
    )(*args)


def swap(value, mask, devices):
    return lax.ppermute(value, "seq", [(i, i ^ mask) for i in range(devices)])


def after(value, *earlier):
    return lax.optimization_barrier((value, earlier))[0]


def share(parts, devices):
    return [parts[0]] + [swap(parts[side], side, devices) for side in range(1, PLANE)]


def spread_out(shared, devices):
    return [
        swap(jnp.concatenate([one[k : k + 1] for one in shared], axis=0), PLANE * k, devices)
        for k in range(1, devices // PLANE)
    ]


def all_to_all(sent):
    return lax.all_to_all(sent, "seq", split_axis=0, concat_axis=0, tiled=True)


def fast_on_device(proj, short_weight, residues, rates, skip, grad_out):
    devices = lax.axis_size("seq")
    rows, channels = grad_out.shape
    modes = rates.shape[0]
    width = channels // 2
    me = lax.axis_index("seq")
    where = jnp.stack([me // PLANE, me % PLANE]).astype(jnp.int32)
    before = lax.ppermute(
        proj[rows - HALO :], "seq", [(i, i + 1) for i in range(devices - 1)]
    )
    streams = (proj, before, short_weight, grad_out)
    partly = mix_streams(where, proj, proj, short_weight, grad_out, 0, 2, devices, True)
    (sent,), query_a, mixed_a = mix_streams(
        where, *streams, 0, 2, devices, True, top=2 * HALO, earlier=(*partly[0], *partly[1:])
    )
    arrived = all_to_all(sent)
    parts, query_b, mixed_b = mix_streams(after(where, sent), *streams, 1, 2, devices, False)
    shared = share(parts, devices)
    tables = spectral_tables(devices, rows, parts[0])
    rates, residues, skip = after((rates, residues, skip), parts)
    decay = jnp.exp(-rates)
    amplitude = residues * jnp.sqrt(rates)
    tiles = (modes, channels // LANES, LANES)
    params = (decay.reshape(tiles), amplitude.reshape(tiles), skip.reshape(tiles[1:]))
    near_a = near_part(after(mixed_a, tables), *params, 0)
    close = after(shared[:2], near_a)
    moved = spread_out(close, devices)
    distant = after(shared[2:], moved[0])
    moved += spread_out(distant, devices)

    def lags(guard, sources, chunk):
        start = chunk * width + me * LANES
        rate = lax.dynamic_slice_in_dim(rates, start, LANES, 1)
        lead = lax.dynamic_slice_in_dim(amplitude, start, LANES, 1)
        return lag_part(after(where, guard), sources, rate, lead, tables, devices)

    back_a = lags(distant[0], [arrived], 0)
    arrived_a = all_to_all(back_a)
    back_b = lags(back_a, [*shared, *moved], 1)
    arrived_b = all_to_all(back_b)
    near_b = near_part(after(mixed_b, back_b), *params, 1)
    result = finish_part(arrived_a, near_a, query_a, decay, None, 0, 2)
    result = finish_part(arrived_b, near_b, query_b, decay, result, 1, 2)
    return tuple(result)


def solution(mesh):
    def body(proj, short_weight, residues, rates, skip, grad_out):
        devices = lax.axis_size("seq")
        rows, channels = grad_out.shape
        fits = (
            devices in (8, 16)
            and rows % LANES == 0
            and channels == 2 * devices * LANES
            and residues.shape[0] == 16
            and short_weight.shape[0] <= HALO + 1
        )
        chosen = fast_on_device if fits else on_device
        return chosen(proj, short_weight, residues, rates, skip, grad_out)

    return jax.shard_map(
        body,
        mesh=mesh,
        in_specs=(P(("groups", "seq"), None), P(), P(), P(), P(), P(("groups", "seq"), None)),
        out_specs=(P(("groups", "seq"), None), P(("groups", "seq"), None)),
        check_vma=False,
    )
```
